128 devices in a mesh: replica: 4 (over x_lo, core), expert: 32 (over x_hi, z, y).
Axes of the slice: x: 4 (x_hi: 2, x_lo: 2; x = x_hi * 2 + x_lo), y: 4, z: 4, core: 2. Of those that a mesh axis runs over, the one named last changes fastest.
Arguments:
- tokens: bfloat16 [16384, 2048], P(('replica', 'expert')), may hold values from -6 to 6
- routing: int32 [16384, 8], P(('replica', 'expert')), may hold values from 0 to 31, all different within a row; in each aligned block of 128 rows (0 to 127, 128 to 255, ...) at most 40 rows name the same one
- gate_scores: float32 [16384, 8], P(('replica', 'expert')), may hold values from 0.1 to 1
- cotangent: bfloat16 [16384, 2048], P(('replica', 'expert')), may hold values from -48 to 48
- w_gate: bfloat16 [4, 32, 2048, 384], P('replica', 'expert'), may hold values from -6 to 6
- w_up: bfloat16 [4, 32, 2048, 384], P('replica', 'expert'), may hold values from -6 to 6
- w_down: bfloat16 [4, 32, 384, 2048], P('replica', 'expert'), may hold values from -6 to 6
- mom_gate: bfloat16 [4, 32, 2048, 384], P('replica', 'expert'), may hold values from -3 to 3
- mom_up: bfloat16 [4, 32, 2048, 384], P('replica', 'expert'), may hold values from -3 to 3
- mom_down: bfloat16 [4, 32, 384, 2048], P('replica', 'expert'), may hold values from -3 to 3
- gossip_round: int32 [32], P('expert'), may hold values from 0 to 1
Outputs:
- layer_out: bfloat16 [16384, 2048], P(('replica', 'expert'))
- token_grad: bfloat16 [16384, 2048], P(('replica', 'expert'))
- new_gate: bfloat16 [4, 32, 2048, 384], P('replica', 'expert')
- new_up: bfloat16 [4, 32, 2048, 384], P('replica', 'expert')
- new_down: bfloat16 [4, 32, 384, 2048], P('replica', 'expert')
- new_mom_gate: bfloat16 [4, 32, 2048, 384], P('replica', 'expert')
- new_mom_up: bfloat16 [4, 32, 2048, 384], P('replica', 'expert')
- new_mom_down: bfloat16 [4, 32, 384, 2048], P('replica', 'expert')
The draws below stay inside these ranges and needn't reach their ends.
Inputs may be any that keep to these rules, and one draw needn't show every extreme that they name: `routing`: each token names 8 different experts; among the 128 tokens of one source no expert is named more than 40 times, a bound that some block reaches. `gossip_round`: each expert's round value names the bit distance of that expert's partner in this round.
All inputs are finite; a program needn't handle non-finite values.
Results may differ from the reference program's by a relative error of at most 0.0064.
Values may be sent and summed in bfloat16 or wider, within the bound.
A program may use at most 192 MiB of HBM per device.

```python
import math
import jax
import jax.numpy as jnp
import numpy as np
from jax import lax

D = 2048
F = 384
TOPK = 8
TOK_DEV = 128
EXPERTS = 32
CAP = 40
TOKENS = 16384
N_REPLICA = 4


def plant(result, key, smallest, high):
    longest = result.shape.index(max(result.shape))
    spots = []
    for shift in (0, 1):
        where = [jax.random.randint(jax.random.fold_in(key, axis), (), 0, length) for axis, length in enumerate(result.shape)]
        where[longest] = (where[longest] + shift) % result.shape[longest]
        spots.append(tuple(where))
    return result.at[spots[0]].set(smallest).at[spots[1]].set(high)


def shard_levels(stream_key, dims, shards, low, high):
    def one(position, blocks):
        heights = jax.random.uniform(jax.random.fold_in(jax.random.fold_in(stream_key, 6), position), (blocks,), jnp.float32, low / len(shards), high / len(shards))
        return jnp.repeat(jnp.exp(heights), dims[position] // blocks).reshape((-1,) + (1,) * (len(dims) - position - 1))

    gain = one(*shards[0])
    for cut in shards[1:]:
        gain = gain * one(*cut)
    return gain


def assign_block(own_key, own, number, rows, amount, top, limit, slope):
    order = jax.random.permutation(own_key, amount)
    packed, common = portions_of(amount, rows * top, limit, slope, True), portions_of(amount, rows * top, limit, slope, False)
    places = jnp.arange(amount)

    def named(tallies, offset_by):
        used = int((tallies > 0).sum())
        fixed = max(1, used // 4)
        shifted = fixed + (places - fixed + offset_by * (used - fixed)) % max(1, amount - fixed)
        return jnp.zeros((amount,), jnp.int32).at[order[jnp.where(places < fixed, places, shifted)]].set(jnp.asarray(tallies, jnp.int32))

    tallies = jnp.where(number % 4 == 0, named(packed, number // 4), named(common, number - number // 4 - 1))
    mixed = jax.random.permutation(jax.random.fold_in(own, 3), amount)
    source_of, taker = mixed[0:amount // 2 * 2:2], mixed[1:amount // 2 * 2:2]
    slack = jnp.minimum(tallies[source_of] - 1, limit - tallies[taker]) // 2
    slack = jnp.where((source_of == order[0]) | (taker == order[0]) | (tallies[taker] == 0), 0, jnp.maximum(slack, 0))
    shifted = jax.random.randint(jax.random.fold_in(own, 4), (amount // 2,), 0, 1 << 20) % (slack + 1)
    tallies = tallies.at[source_of].add(-shifted).at[taker].add(shifted)
    items = jnp.searchsorted(jnp.cumsum(tallies), jnp.arange(rows * top), side="right").astype(jnp.int32)
    grid = items.reshape(top, rows).T
    grid = grid[jax.random.permutation(jax.random.fold_in(own, 1), rows)]
    offset_by = jax.random.randint(jax.random.fold_in(own, 2), (rows, 1), 0, top)
    return jnp.take_along_axis(grid, (jnp.arange(top)[None, :] + offset_by) % top, axis=1)


def portions_of(number_of, total, bound, lean, full):
    loads = [(1 << 20) // math.isqrt(standing ** lean) + 1 for standing in range(1, number_of + 1)]
    largest = bound if full else min(bound, max(-(-total // number_of), total * loads[0] // sum(loads)))
    least = 1 if total - largest >= number_of - 1 else 0
    holding, spare = [largest] + [least] * (number_of - 1), total - largest - least * (number_of - 1)
    while spare > 0:
        free = [i for i in range(1, number_of) if holding[i] < largest] or [i for i in range(1, number_of) if holding[i] < bound]
        whole, remaining = sum([loads[i] for i in free]), spare
        for i in free:
            extra = min(bound - holding[i], max(1, remaining * loads[i] // whole), spare)
            holding[i] = holding[i] + extra
            spare = spare - extra
    return np.array(holding)


def noise(stream_key, dims, deviation, most, cuts=(), held_as=jnp.bfloat16):
    entries = jax.random.normal(stream_key, dims, jnp.float32) * deviation
    if len(cuts) > 0:
        entries = shard_levels(stream_key, dims, cuts, -0.22, 0.18) * entries
    return jnp.clip(entries, min=-most, max=most).astype(held_as)


def setup_inputs(seed: int = 0) -> dict:
    streams_of = jax.random.split(jax.random.key(seed), 12)
    tokens = noise(streams_of[0], (TOKENS, D), 1.0, 6.0, ((0, 128),))
    routing_keys = jax.random.split(jax.random.fold_in(streams_of[1], 1), TOKENS // TOK_DEV)
    routing_turns = jax.random.permutation(jax.random.fold_in(streams_of[1], 3), TOKENS // TOK_DEV)
    routing = jax.vmap(lambda own, number: assign_block(jax.random.fold_in(streams_of[1], 2), own, number, TOK_DEV, EXPERTS, TOPK, CAP, 2))(routing_keys, routing_turns).reshape((TOKENS, TOPK))
    gate_scores = jnp.clip(jnp.exp(math.log(1.0) - 2.3025851 * jax.random.uniform(streams_of[2], (TOKENS, TOPK), jnp.float32) ** shard_levels(streams_of[2], (TOKENS, TOPK), ((0, 128),), -0.2, 0.2)), 0.1, 1.0)
    cotangent = noise(streams_of[3], (TOKENS, D), 8.0, 48.0, ((0, 128),))
    w_gate = noise(streams_of[4], (N_REPLICA, EXPERTS, D, F), 1.0, 6.0, ((0, 4), (1, 32)))
    w_up = noise(streams_of[5], (N_REPLICA, EXPERTS, D, F), 1.0, 6.0, ((0, 4), (1, 32)))
    w_down = noise(streams_of[6], (N_REPLICA, EXPERTS, F, D), 1.0, 6.0, ((0, 4), (1, 32)))
    mom_gate = noise(streams_of[7], (N_REPLICA, EXPERTS, D, F), 0.5, 3.0, ((0, 4), (1, 32)))
    mom_up = noise(streams_of[8], (N_REPLICA, EXPERTS, D, F), 0.5, 3.0, ((0, 4), (1, 32)))
    mom_down = noise(streams_of[9], (N_REPLICA, EXPERTS, F, D), 0.5, 3.0, ((0, 4), (1, 32)))
    gossip_round = plant(jax.random.randint(streams_of[10], (EXPERTS,), 0, 2), jax.random.fold_in(streams_of[10], 1), 0, 1).astype(jnp.int32)
    return dict(tokens=tokens, routing=routing, gate_scores=gate_scores, cotangent=cotangent, w_gate=w_gate, w_up=w_up, w_down=w_down, mom_gate=mom_gate, mom_up=mom_up, mom_down=mom_down, gossip_round=gossip_round)


momentum_beta = 0.9
learn_rate = 0.1


def expert_forward(rows_in, weight_gate, weight_up, weight_down):
    scale_in = rows_in.shape[1] ** -0.5
    scale_hidden = weight_gate.shape[1] ** -0.5
    gate_pre = jnp.dot(rows_in, weight_gate, preferred_element_type=jnp.float32) * scale_in
    up_pre = jnp.dot(rows_in, weight_up, preferred_element_type=jnp.float32) * scale_in
    sigmoid_gate = jax.nn.sigmoid(gate_pre)
    activation = (gate_pre * sigmoid_gate * up_pre).astype(jnp.bfloat16)
    produced = (jnp.dot(activation, weight_down, preferred_element_type=jnp.float32) * scale_hidden).astype(jnp.bfloat16)
    return gate_pre, up_pre, sigmoid_gate, activation, produced


def expert_backward(rows_in, rows_grad, weight_gate, weight_up, weight_down, gate_pre, up_pre, sigmoid_gate, activation):
    scale_in = rows_in.shape[1] ** -0.5
    scale_hidden = weight_gate.shape[1] ** -0.5
    inner_dims = (((1,), (1,)), ((), ()))
    outer_dims = (((0,), (0,)), ((), ()))
    grad_act = lax.dot_general(rows_grad, weight_down, inner_dims, preferred_element_type=jnp.float32) * scale_hidden
    grad_gate_pre = (grad_act * up_pre * sigmoid_gate * (1.0 + gate_pre * (1.0 - sigmoid_gate))).astype(jnp.bfloat16)
    grad_up_pre = (grad_act * gate_pre * sigmoid_gate).astype(jnp.bfloat16)
    grad_down = lax.dot_general(activation, rows_grad, outer_dims, preferred_element_type=jnp.float32) * scale_hidden
    grad_gate = lax.dot_general(rows_in, grad_gate_pre, outer_dims, preferred_element_type=jnp.float32) * scale_in
    grad_up = lax.dot_general(rows_in, grad_up_pre, outer_dims, preferred_element_type=jnp.float32) * scale_in
    back_sum = lax.dot_general(grad_gate_pre, weight_gate, inner_dims, preferred_element_type=jnp.float32)
    back_sum = back_sum + lax.dot_general(grad_up_pre, weight_up, inner_dims, preferred_element_type=jnp.float32)
    rows_back = (back_sum * scale_in).astype(jnp.bfloat16)
    return rows_back, grad_gate, grad_up, grad_down


def momentum_step(weight, moment, gradient):
    moment_new = momentum_beta * moment.astype(jnp.float32) + gradient
    weight_new = (weight.astype(jnp.float32) - learn_rate * moment_new).astype(jnp.bfloat16)
    return weight_new, moment_new.astype(jnp.bfloat16)


def reference(tokens, routing, gate_scores, cotangent, w_gate, w_up, w_down, mom_gate, mom_up, mom_down, gossip_round):
    sources = EXPERTS
    pair_count = TOK_DEV * TOPK
    outs_list = []
    grads_list = []
    local_lists = [[], [], [], [], [], []]
    token_of = jnp.arange(pair_count, dtype=jnp.int32) // TOPK
    source_ids = jnp.broadcast_to(jnp.arange(sources, dtype=jnp.int32)[:, None], (sources, pair_count))
    for replica_id in range(N_REPLICA):
        first = replica_id * sources * TOK_DEV
        tok_block = tokens[first:first + sources * TOK_DEV].reshape(sources, TOK_DEV, D)
        cot_block = cotangent[first:first + sources * TOK_DEV].reshape(sources, TOK_DEV, D)
        scores = gate_scores[first:first + sources * TOK_DEV].reshape(sources, TOK_DEV, TOPK)
        gate_share = (scores / jnp.sum(scores, axis=2, keepdims=True)).reshape(sources, pair_count)
        expert_ids = routing[first:first + sources * TOK_DEV].reshape(sources, pair_count)
        member = (expert_ids[:, :, None] == jnp.arange(EXPERTS, dtype=jnp.int32)[None, None, :]).astype(jnp.int32)
        earlier = jnp.sum((jnp.cumsum(member, axis=1) - member) * member, axis=2).astype(jnp.int32)
        pair_rows = tok_block[:, token_of]
        pair_grad = (gate_share[:, :, None] * cot_block[:, token_of].astype(jnp.float32)).astype(jnp.bfloat16)
        buffer_x = jnp.zeros((EXPERTS, sources, CAP, D), jnp.bfloat16).at[expert_ids, source_ids, earlier].set(pair_rows)
        buffer_g = jnp.zeros((EXPERTS, sources, CAP, D), jnp.bfloat16).at[expert_ids, source_ids, earlier].set(pair_grad)
        buffer_x = buffer_x.reshape(EXPERTS, sources * CAP, D)
        buffer_g = buffer_g.reshape(EXPERTS, sources * CAP, D)

        def per_expert(items):
            rows_in, rows_grad, weight_gate, weight_up, weight_down, moment_gate, moment_up, moment_down = items
            gate_pre, up_pre, sigmoid_gate, activation, produced = expert_forward(rows_in, weight_gate, weight_up, weight_down)
            rows_back, grad_gate, grad_up, grad_down = expert_backward(rows_in, rows_grad, weight_gate, weight_up, weight_down, gate_pre, up_pre, sigmoid_gate, activation)
            gate_new, gate_moment = momentum_step(weight_gate, moment_gate, grad_gate)
            up_new, up_moment = momentum_step(weight_up, moment_up, grad_up)
            down_new, down_moment = momentum_step(weight_down, moment_down, grad_down)
            return produced, rows_back, gate_new, up_new, down_new, gate_moment, up_moment, down_moment

        results = lax.map(per_expert, (buffer_x, buffer_g, w_gate[replica_id], w_up[replica_id], w_down[replica_id], mom_gate[replica_id], mom_up[replica_id], mom_down[replica_id]))
        produced_all = results[0].reshape(EXPERTS, sources, CAP, D)
        back_all = results[1].reshape(EXPERTS, sources, CAP, D)
        picked = produced_all[expert_ids, source_ids, earlier].astype(jnp.float32)
        picked_back = back_all[expert_ids, source_ids, earlier].astype(jnp.float32)
        mixed_rows = jnp.sum((picked * gate_share[:, :, None]).reshape(sources, TOK_DEV, TOPK, D), axis=2)
        back_rows = jnp.sum(picked_back.reshape(sources, TOK_DEV, TOPK, D), axis=2)
        outs_list.append(mixed_rows.astype(jnp.bfloat16).reshape(sources * TOK_DEV, D))
        grads_list.append(back_rows.astype(jnp.bfloat16).reshape(sources * TOK_DEV, D))
        for index_item in range(6):
            local_lists[index_item].append(results[2 + index_item])
    layer_out = jnp.concatenate(outs_list, axis=0)
    token_grad = jnp.concatenate(grads_list, axis=0)
    bit_count = N_REPLICA.bit_length() - 1
    bit_now = (gossip_round % bit_count).astype(jnp.int32)
    replica_ids = jnp.arange(N_REPLICA, dtype=jnp.int32)[:, None]
    partner_ids = jnp.bitwise_xor(replica_ids, jnp.left_shift(jnp.ones((), jnp.int32), bit_now)[None, :]).astype(jnp.int32)
    expert_index = jnp.broadcast_to(jnp.arange(EXPERTS, dtype=jnp.int32)[None, :], (N_REPLICA, EXPERTS))
    averaged = []
    for index_item in range(3):
        stacked_local = jnp.stack(local_lists[index_item], axis=0)
        partner_w = stacked_local[partner_ids, expert_index]
        averaged.append(((stacked_local.astype(jnp.float32) + partner_w.astype(jnp.float32)) * 0.5).astype(jnp.bfloat16))
    moments = [jnp.stack(local_lists[3 + index_item], axis=0) for index_item in range(3)]
    return (layer_out, token_grad, averaged[0], averaged[1], averaged[2], moments[0], moments[1], moments[2])
```

```python
import jax
import jax.numpy as jnp
from jax import lax
from jax.experimental import pallas as pl
from jax.experimental.pallas import tpu as pltpu
from jax.sharding import PartitionSpec as P

momentum_beta = 0.9
learn_rate = 0.1
MESH = pl.DeviceIdType.MESH
CAP = 40
BF = jnp.bfloat16
F32 = jnp.float32
ORDER = (1, 3, 2)


def place():
    e = lax.axis_index("expert")
    return e // 16, (e // 4) % 4, e % 4


def number(xh, z, y):
    return xh * 16 + z * 4 + y


def peer(route, stage, xh, z, y, d):
    if (route == 0) == (stage == 0):
        return number(xh, z, (y + d) % 4)
    return number(xh, (z + d) % 4, y)


def greet(ids):
    barrier = pltpu.get_barrier_semaphore()
    for where in ids:
        pl.semaphore_signal(barrier, inc=1, device_id=where, device_id_type=MESH)
    pl.semaphore_wait(barrier, len(ids))


def remote(src, dst, ss, rs, where):
    return pltpu.make_async_remote_copy(
        src_ref=src, dst_ref=dst, send_sem=ss, recv_sem=rs, device_id=where, device_id_type=MESH
    )


def turn(i):
    return i + i // 2 - 2 * (i // 3)


def selection(meta, route, group):
    width = 128
    rows = lax.broadcasted_iota(jnp.int32, (2 * CAP, width), 0).astype(F32)
    first = meta[route, group, 0]
    second = meta[route, group, 1]
    hits, shares = [], []
    for e in range(4):
        hit = jnp.concatenate(
            [rows == first[e : e + 1, :], rows == second[e : e + 1, :] + float(CAP)], axis=1
        )
        share = jnp.concatenate([first[4 + e : 5 + e, :], second[4 + e : 5 + e, :]], axis=1)
        hits.append(hit)
        shares.append(jnp.where(hit, share, 0.0))
    hit = jnp.concatenate([jnp.where(h, 1.0, 0.0) for h in hits], axis=0)
    return hit, jnp.concatenate(shares, axis=0)


def dispatch_kernel(
    tok, cot, m1, m2, xo, yo, mo,
    ag, sb, xb, mr,
    ms, mrs, xs, xr, gs, gr, us, ur, ls, lo, os_,
):
    xh, z, y = place()
    half = ag.shape[-1]
    others = []
    for dx in range(2):
        for d in range(4):
            if dx or d:
                others.append({"expert": number((xh + dx) % 2, z, (y + d) % 4)})
            if d:
                others.append({"expert": number((xh + dx) % 2, (z + d) % 4, y)})
    greet(others)
    own = (y, z)
    source = (tok, cot)
    partner = {"expert": number(1 - xh, z, y)}

    def cols(a, r):
        return source[a].at[:, pl.ds(r * half, half)]

    def x_copy(a, r):
        spot = ag.at[a, r, own[r], pl.ds(xh * 128, 128)]
        return remote(cols(a, r), spot, xs.at[a, r], xr.at[a, r], partner)

    def own_copy(a, r):
        return pltpu.make_async_copy(
            cols(a, r), ag.at[a, r, own[r], pl.ds(xh * 128, 128)], ls.at[a, r]
        )

    def gather_copy(a, r, h, d):
        where = xh if h == 0 else 1 - xh
        spot = ag.at[a, r, own[r], pl.ds(where * 128, 128)]
        src = cols(a, r) if h == 0 else spot
        return remote(
            src, spot, gs.at[a, r, h, d], gr.at[a, r, h, d],
            {"expert": peer(r, 0, xh, z, y, d)},
        )

    def gather_wait(a, r, h, q):
        where = xh if h == 0 else 1 - xh
        spot = ag.at[a, r, (own[r] + q) % 4, pl.ds(where * 128, 128)]
        back = (4 - q) % 4
        remote(spot, spot, gs.at[a, r, h, back], gr.at[a, r, h, back], partner).wait_recv()

    def landing(a, r, sender, group):
        return xb.at[a, r, sender, group] if r == 0 else xb.at[a, r, group, sender]

    def spread_copy(a, r, q, d):
        group = (own[r] + q) % 4
        me = own[1 - r]
        return remote(
            sb.at[a, r, (me + d) % 4, q], landing(a, r, me, group),
            us.at[a, r, q, d], ur.at[a, r, q, d],
            {"expert": peer(r, 1, xh, z, y, d)},
        )

    def keep_copy(a, r, q):
        group = (own[r] + q) % 4
        me = own[1 - r]
        return pltpu.make_async_copy(sb.at[a, r, me, q], landing(a, r, me, group), lo.at[a, r, q])

    metas = (m1, m2)
    for r in range(2):
        mr[r, own[r], xh] = metas[r][xh, own[r]]

    def meta_copy(r, dx, d):
        to_x = (xh + dx) % 2
        to = (own[r] + d) % 4
        where = number(to_x, z, to) if r == 0 else number(to_x, to, y)
        return remote(
            metas[r].at[to_x, to], mr.at[r, own[r], xh], ms.at[r, dx, d], mrs.at[r, dx, d],
            {"expert": where},
        )

    pairs = [(dx, d) for dx in range(2) for d in range(4) if dx or d]
    for r in range(2):
        for dx, d in pairs:
            meta_copy(r, dx, d).start()
    for r in range(2):
        x_copy(0, r).start()
        own_copy(0, r).start()
    for d in ORDER:
        for r in range(2):
            gather_copy(0, r, 0, d).start()
    for r in range(2):
        x_copy(1, r).start()
        own_copy(1, r).start()

    def pass_on(a):
        for r in range(2):
            own_copy(a, r).wait()
            spot = ag.at[a, r, own[r], pl.ds((1 - xh) * 128, 128)]
            remote(spot, spot, xs.at[a, r], xr.at[a, r], partner).wait_recv()
            for d in ORDER:
                gather_copy(a, r, 1, d).start()

    pass_on(0)
    for d in ORDER:
        for r in range(2):
            gather_copy(1, r, 0, d).start()
    for r in range(2):
        for dx, d in pairs:
            meta_copy(r, dx, d).wait()

    def spread(a):
        def body(i, carry):
            q = turn(i)
            for r in range(2):
                group = (own[r] + q) % 4

                @pl.when(i > 0)
                def _():
                    gather_wait(a, r, 0, q)
                    gather_wait(a, r, 1, q)

                hit, share = selection(mr, r, group)
                hit = hit.astype(BF)
                for c in range(2):
                    part = pl.ds(c * (half // 2), half // 2)
                    rows = jnp.dot(hit, ag[a, r, group, :, part], preferred_element_type=F32)
                    if a == 1:
                        rows = rows * jnp.sum(share, axis=1, keepdims=True)
                    rows = rows.astype(BF)
                    for e in range(4):
                        sb[a, r, e, q, :, part] = rows[e * 80 : e * 80 + 80]
                for d in ORDER:
                    spread_copy(a, r, q, d).start()
                keep_copy(a, r, q).start()
            return carry

        lax.fori_loop(0, 4, body, 0)

    spread(0)
    pass_on(1)
    spread(1)
    results = (xo, yo)

    def finish(a):
        for r in range(2):
            for q in range(4):
                keep_copy(a, r, q).wait()
                for d in ORDER:
                    spread_copy(a, r, q, d).wait()
            for g in range(4):
                for k in range(4):
                    pltpu.make_async_copy(
                        xb.at[a, r, g, k],
                        results[a].at[pl.ds((g * 4 + k) * 80, 80), pl.ds(r * half, half)],
                        os_.at[a, r, g, k],
                    ).start()

    finish(0)
    finish(1)
    mo[...] = mr[...]
    for a in range(2):
        for r in range(2):
            x_copy(a, r).wait_send()
            for h in range(2):
                for d in ORDER:
                    gather_copy(a, r, h, d).wait_send()
            for g in range(4):
                for k in range(4):
                    pltpu.make_async_copy(
                        xb.at[a, r, g, k],
                        results[a].at[pl.ds((g * 4 + k) * 80, 80), pl.ds(r * half, half)],
                        os_.at[a, r, g, k],
                    ).wait()


def dispatch(tokens, cotangent, m1, m2):
    rows, width = tokens.shape
    half = width // 2
    dma = pltpu.SemaphoreType.DMA
    anywhere = pl.BlockSpec(memory_space=pl.ANY)
    vmem = pl.BlockSpec(memory_space=pltpu.VMEM)
    return pl.pallas_call(
        dispatch_kernel,
        out_shape=(
            jax.ShapeDtypeStruct((32 * CAP, width), BF),
            jax.ShapeDtypeStruct((32 * CAP, width), BF),
            jax.ShapeDtypeStruct((2, 4, 2, 8, 128), F32),
        ),
        in_specs=[anywhere, anywhere, vmem, vmem],
        out_specs=(anywhere, anywhere, vmem),
        scratch_shapes=[
            pltpu.VMEM((2, 2, 4, 256, half), BF),
            pltpu.VMEM((2, 2, 4, 4, 80, half), BF),
            pltpu.VMEM((2, 2, 4, 4, 80, half), BF),
            pltpu.VMEM((2, 4, 2, 8, 128), F32),
            dma((2, 2, 4)), dma((2, 2, 4)),
            dma((2, 2)), dma((2, 2)),
            dma((2, 2, 2, 4)), dma((2, 2, 2, 4)),
            dma((2, 2, 4, 4)), dma((2, 2, 4, 4)),
            dma((2, 2)), dma((2, 2, 4)), dma((2, 2, 4, 4)),
        ],
        compiler_params=pltpu.CompilerParams(
            collective_id=0, has_side_effects=True, vmem_limit_bytes=60 * 2**20
        ),
        name="dispatch",
    )(tokens, cotangent, m1, m2)


def combine_kernel(
    pr, bk, mr, lg, lu, ld,
    out, tg, bg0, bu0, bd0, bg1, bu1, bd1,
    rb, qs, qr, xsend, xrecv, mine,
    cs, cr, ls, ps, pt, xs, xr, ws, wr,
):
    xh, z, y = place()
    rep = lax.axis_index("replica")
    half = rb.shape[-1]
    own = (y, z)
    partner = {"expert": number(1 - xh, z, y)}
    core_mate = {"replica": rep + 1 - 2 * (rep % 2)}
    far_mate = {"replica": (rep + 2) % 4}
    others = [partner, core_mate, far_mate]
    for d in ORDER:
        others.append({"expert": number(xh, z, (y + d) % 4)})
        others.append({"expert": number(xh, (z + d) % 4, y)})
    greet(others)
    source = (pr, bk)
    results = (out, tg)

    def block(a, r, e, group):
        row = (e * 4 + group) if r == 0 else (group * 4 + e)
        return source[a].at[pl.ds(row * 80, 80), pl.ds(r * half, half)]

    def send_copy(a, r, q, d):
        group = (own[r] + q) % 4
        me = own[1 - r]
        return remote(
            block(a, r, (me + d) % 4, group), rb.at[a, r, group, me],
            cs.at[a, r, q, d], cr.at[a, r, q, d],
            {"expert": peer(r, 1, xh, z, y, d)},
        )

    def keep_copy(a, r, q):
        group = (own[r] + q) % 4
        me = own[1 - r]
        return pltpu.make_async_copy(block(a, r, me, group), rb.at[a, r, group, me], ls.at[a, r, q])

    def part_copy(a, r, q):
        return remote(
            qs.at[a, r, q], qr.at[a, r, q], ps.at[a, r, q], pt.at[a, r, q],
            {"expert": peer(r, 0, xh, z, y, q)},
        )

    def x_copy(a, r):
        return remote(xsend.at[a, r], xrecv.at[a, r], xs.at[a, r], xr.at[a, r], partner)

    weights = ((lg, bg0, bg1), (lu, bu0, bu1), (ld, bd0, bd1))
    swaps = []
    for i, (w, b0, b1) in enumerate(weights):
        swaps.append(remote(w, b1, ws.at[1, i], wr.at[1, i], far_mate))
        swaps.append(remote(w, b0, ws.at[0, i], wr.at[0, i], core_mate))
    for s in swaps:
        s.start()
    for a in range(2):
        for q in (1, 3, 2, 0):
            for r in range(2):
                keep_copy(a, r, q).start()
            for d in ORDER:
                for r in range(2):
                    send_copy(a, r, q, d).start()

    def reduce(a):
        def body(i, carry):
            q = turn((i + 1) % 4)
            for r in range(2):
                group = (own[r] + q) % 4
                keep_copy(a, r, q).wait()
                for d in ORDER:
                    send_copy(a, r, q, d).wait_recv()
                hit, share = selection(mr, r, group)
                pick = (share if a == 0 else hit).astype(BF)
                for c in range(2):
                    part = pl.ds(c * (half // 2), half // 2)
                    rows = jnp.concatenate([rb[a, r, group, e, :, part] for e in range(4)], axis=0)
                    total = lax.dot_general(
                        pick, rows, (((0,), (0,)), ((), ())), preferred_element_type=F32
                    )

                    @pl.when(i < 3)
                    def _():
                        qs[a, r, q, :, part] = total.astype(BF)

                    @pl.when(i == 3)
                    def _():
                        mine[r, :, part] = total

                @pl.when(i < 3)
                def _():
                    part_copy(a, r, q).start()
            return carry

        lax.fori_loop(0, 4, body, 0)
        there = pl.ds((1 - xh) * 128, 128)
        here = pl.ds(xh * 128, 128)
        for r in range(2):
            for q in ORDER:
                part_copy(a, r, q).wait_recv()
            away = mine[r, there]
            stay = mine[r, here]
            for q in ORDER:
                away = away + qr[a, r, q, there].astype(F32)
                stay = stay + qr[a, r, q, here].astype(F32)
            xsend[a, r] = away.astype(BF)
            x_copy(a, r).start()
            mine[2 + 2 * a + r, pl.ds(0, 128)] = stay

    reduce(0)
    reduce(1)
    for a in range(2):
        for r in range(2):
            x_copy(a, r).wait_recv()
            total = mine[2 + 2 * a + r, pl.ds(0, 128)] + xrecv[a, r].astype(F32)
            results[a][:, pl.ds(r * half, half)] = total.astype(BF)
    for a in range(2):
        for r in range(2):
            x_copy(a, r).wait_send()
            for q in range(4):
                for d in ORDER:
                    send_copy(a, r, q, d).wait_send()
            for q in ORDER:
                part_copy(a, r, q).wait_send()
    for s in swaps:
        s.wait()


def combine(produced, rows_back, meta, lg, lu, ld):
    width = produced.shape[1]
    half = width // 2
    dma = pltpu.SemaphoreType.DMA
    anywhere = pl.BlockSpec(memory_space=pl.ANY)
    vmem = pl.BlockSpec(memory_space=pltpu.VMEM)
    tokens = jax.ShapeDtypeStruct((128, width), BF)
    weights = [jax.ShapeDtypeStruct(w.shape, w.dtype) for w in (lg, lu, ld)]
    return pl.pallas_call(
        combine_kernel,
        out_shape=(tokens, tokens, *weights, *weights),
        in_specs=[anywhere, anywhere, vmem, anywhere, anywhere, anywhere],
        out_specs=(vmem, vmem, *[anywhere] * 6),
        scratch_shapes=[
            pltpu.VMEM((2, 2, 4, 4, 80, half), BF),
            pltpu.VMEM((2, 2, 4, 256, half), BF),
            pltpu.VMEM((2, 2, 4, 256, half), BF),
            pltpu.VMEM((2, 2, 128, half), BF),
            pltpu.VMEM((2, 2, 128, half), BF),
            pltpu.VMEM((6, 256, half), F32),
            dma((2, 2, 4, 4)), dma((2, 2, 4, 4)),
            dma((2, 2, 4)),
            dma((2, 2, 4)), dma((2, 2, 4)),
            dma((2, 2)), dma((2, 2)),
            dma((2, 3)), dma((2, 3)),
        ],
        compiler_params=pltpu.CompilerParams(
            collective_id=1, has_side_effects=True, vmem_limit_bytes=60 * 2**20
        ),
        name="combine",
    )(produced, rows_back, meta, lg, lu, ld)


def expert_math(rows_in, rows_grad, weight_gate, weight_up, weight_down):
    scale_in = rows_in.shape[1] ** (-0.5)
    scale_hidden = weight_gate.shape[1] ** (-0.5)
    inner = (((1,), (1,)), ((), ()))
    outer = (((0,), (0,)), ((), ()))
    gate_pre = jnp.dot(rows_in, weight_gate, preferred_element_type=F32) * scale_in
    up_pre = jnp.dot(rows_in, weight_up, preferred_element_type=F32) * scale_in
    sig = jax.nn.sigmoid(gate_pre)
    activation = (gate_pre * sig * up_pre).astype(BF)
    produced = (jnp.dot(activation, weight_down, preferred_element_type=F32) * scale_hidden).astype(BF)
    grad_act = lax.dot_general(rows_grad, weight_down, inner, preferred_element_type=F32) * scale_hidden
    grad_gate_pre = (grad_act * up_pre * sig * (1.0 + gate_pre * (1.0 - sig))).astype(BF)
    grad_up_pre = (grad_act * gate_pre * sig).astype(BF)
    grad_down = lax.dot_general(activation, rows_grad, outer, preferred_element_type=F32) * scale_hidden
    grad_gate = lax.dot_general(rows_in, grad_gate_pre, outer, preferred_element_type=F32) * scale_in
    grad_up = lax.dot_general(rows_in, grad_up_pre, outer, preferred_element_type=F32) * scale_in
    back = lax.dot_general(grad_gate_pre, weight_gate, inner, preferred_element_type=F32)
    back = back + lax.dot_general(grad_up_pre, weight_up, inner, preferred_element_type=F32)
    rows_back = (back * scale_in).astype(BF)
    return produced, rows_back, grad_gate, grad_up, grad_down


def momentum_step(weight, moment, gradient):
    moment_new = momentum_beta * moment.astype(F32) + gradient
    weight_new = (weight.astype(F32) - learn_rate * moment_new).astype(BF)
    return weight_new, moment_new.astype(BF)


def metadata(routing, gate_scores):
    share = gate_scores / jnp.sum(gate_scores, axis=1, keepdims=True)
    count = routing.shape[0]
    names = routing.T[:, None, :] == jnp.arange(32, dtype=jnp.int32)[None, :, None]
    member = jnp.any(names, axis=0)
    shares = jnp.sum(jnp.where(names, share.T[:, None, :], 0.0), axis=0)
    spot = jnp.arange(count, dtype=jnp.int32)
    before = (spot[:, None] < spot[None, :]).astype(BF)
    earlier = jnp.dot(member.astype(BF), before, preferred_element_type=F32)
    slots = jnp.where(member, earlier, -1000.0).reshape(2, 4, 4, count)
    shares = shares.reshape(2, 4, 4, count)
    m2 = jnp.concatenate([slots, shares], axis=2)
    m1 = jnp.concatenate([slots.transpose(0, 2, 1, 3), shares.transpose(0, 2, 1, 3)], axis=2)
    return m1, m2


def per_device(
    tokens, routing, gate_scores, cotangent,
    w_gate, w_up, w_down, mom_gate, mom_up, mom_down, gossip_round,
):
    m1, m2 = metadata(routing, gate_scores)
    rows_in, rows_grad, meta = dispatch(tokens, cotangent, m1, m2)
    weight_gate, weight_up, weight_down = w_gate[0, 0], w_up[0, 0], w_down[0, 0]
    produced, rows_back, grad_gate, grad_up, grad_down = expert_math(
        rows_in, rows_grad, weight_gate, weight_up, weight_down
    )
    gate_new, gate_moment = momentum_step(weight_gate, mom_gate[0, 0], grad_gate)
    up_new, up_moment = momentum_step(weight_up, mom_up[0, 0], grad_up)
    down_new, down_moment = momentum_step(weight_down, mom_down[0, 0], grad_down)
    layer_out, token_grad, *swapped = combine(
        produced, rows_back, meta, gate_new, up_new, down_new
    )
    near = gossip_round[0] % 2 == 0
    averaged = []
    for i, local in enumerate((gate_new, up_new, down_new)):
        other = jnp.where(near, swapped[i].astype(F32), swapped[3 + i].astype(F32))
        averaged.append(((local.astype(F32) + other) * 0.5).astype(BF)[None, None])
    return (
        layer_out, token_grad, *averaged,
        gate_moment[None, None], up_moment[None, None], down_moment[None, None],
    )


def solution(mesh):
    flat = P(("replica", "expert"), None)
    stacked = P("replica", "expert", None, None)
    return jax.shard_map(
        per_device,
        mesh=mesh,
        in_specs=(flat,) * 4 + (stacked,) * 6 + (P("expert"),),
        out_specs=(flat,) * 2 + (stacked,) * 6,
        check_vma=False,
    )
```

```python
import jax
import jax.numpy as jnp
from jax import lax
from jax.experimental import pallas as pl
from jax.experimental.pallas import tpu as pltpu
from jax.sharding import PartitionSpec as P

momentum_beta = 0.9
learn_rate = 0.1
MESH = pl.DeviceIdType.MESH
CAP = 40
BF = jnp.bfloat16
F32 = jnp.float32
ORDER = (1, 3, 2)


def place():
    e = lax.axis_index("expert")
    return e // 16, (e // 4) % 4, e % 4


def number(xh, z, y):
    return xh * 16 + z * 4 + y


def peer(route, stage, xh, z, y, d):
    if (route == 0) == (stage == 0):
        return number(xh, z, (y + d) % 4)
    return number(xh, (z + d) % 4, y)


def greet(ids):
    barrier = pltpu.get_barrier_semaphore()
    for where in ids:
        pl.semaphore_signal(barrier, inc=1, device_id=where, device_id_type=MESH)
    pl.semaphore_wait(barrier, len(ids))


def remote(src, dst, ss, rs, where):
    return pltpu.make_async_remote_copy(
        src_ref=src, dst_ref=dst, send_sem=ss, recv_sem=rs, device_id=where, device_id_type=MESH
    )


def turn(i):
    return i + i // 2 - 2 * (i // 3)


def selection(meta, route, group):
    width = 128
    rows = lax.broadcasted_iota(jnp.int32, (2 * CAP, width), 0).astype(F32)
    first = meta[route, group, 0]
    second = meta[route, group, 1]
    hits, shares = [], []
    for e in range(4):
        hit = jnp.concatenate(
            [rows == first[e : e + 1, :], rows == second[e : e + 1, :] + float(CAP)], axis=1
        )
        share = jnp.concatenate([first[4 + e : 5 + e, :], second[4 + e : 5 + e, :]], axis=1)
        hits.append(hit)
        shares.append(jnp.where(hit, share, 0.0))
    hit = jnp.concatenate([jnp.where(h, 1.0, 0.0) for h in hits], axis=0)
    return hit, jnp.concatenate(shares, axis=0)


def metadata(rt, gt, m1, m2):
    share = gt[...] / jnp.sum(gt[...], axis=0, keepdims=True)
    names = lax.broadcasted_iota(jnp.int32, (32, 128), 0)
    member = jnp.zeros((32, 128), F32)
    shares = jnp.zeros((32, 128), F32)
    for k in range(8):
        same = rt[k : k + 1, :] == names
        member = member + jnp.where(same, 1.0, 0.0)
        shares = shares + jnp.where(same, share[k : k + 1, :], 0.0)
    earlier_token = lax.broadcasted_iota(jnp.int32, (128, 128), 0)
    later_token = lax.broadcasted_iota(jnp.int32, (128, 128), 1)
    before = jnp.where(earlier_token < later_token, 1.0, 0.0).astype(BF)
    earlier = jnp.dot(member.astype(BF), before, preferred_element_type=F32)
    slots = jnp.where(member > 0.0, earlier, -1000.0)
    for xh in range(2):
        for i in range(4):
            for k in range(4):
                e1 = xh * 16 + k * 4 + i
                e2 = xh * 16 + i * 4 + k
                m1[xh, i, k : k + 1, :] = slots[e1 : e1 + 1]
                m1[xh, i, 4 + k : 5 + k, :] = shares[e1 : e1 + 1]
                m2[xh, i, k : k + 1, :] = slots[e2 : e2 + 1]
                m2[xh, i, 4 + k : 5 + k, :] = shares[e2 : e2 + 1]


def dispatch_kernel(
    tok, cot, rt, gt, wg, wu, wd,
    xo, yo, po, guo, aco, mo,
    ag, sb, xb, mr, m1, m2, wgu, wdn, gus, acs, prs,
    ms, mrs, xs, xr, gs, gr, us, ur, ls, lo, os_, wl, fo,
):
    xh, z, y = place()
    half = ag.shape[-1]
    hidden = wd.shape[0]
    scale_in = (2 * half) ** (-0.5)
    scale_hidden = hidden ** (-0.5)
    loads = [
        pltpu.make_async_copy(wg, wgu.at[:, pl.ds(0, hidden)], wl.at[0]),
        pltpu.make_async_copy(wu, wgu.at[:, pl.ds(hidden, hidden)], wl.at[1]),
        pltpu.make_async_copy(wd, wdn, wl.at[2]),
    ]
    others = []
    for dx in range(2):
        for d in range(4):
            if dx or d:
                others.append({"expert": number((xh + dx) % 2, z, (y + d) % 4)})
            if d:
                others.append({"expert": number((xh + dx) % 2, (z + d) % 4, y)})
    greet(others)
    own = (y, z)
    source = (tok, cot)
    partner = {"expert": number(1 - xh, z, y)}

    def cols(a, r):
        return source[a].at[:, pl.ds(r * half, half)]

    def x_copy(a, r):
        spot = ag.at[a, r, own[r], pl.ds(xh * 128, 128)]
        return remote(cols(a, r), spot, xs.at[a, r], xr.at[a, r], partner)

    def own_copy(a, r):
        return pltpu.make_async_copy(
            cols(a, r), ag.at[a, r, own[r], pl.ds(xh * 128, 128)], ls.at[a, r]
        )

    def gather_copy(a, r, h, d):
        where = xh if h == 0 else 1 - xh
        spot = ag.at[a, r, own[r], pl.ds(where * 128, 128)]
        src = cols(a, r) if h == 0 else spot
        return remote(
            src, spot, gs.at[a, r, h, d], gr.at[a, r, h, d],
            {"expert": peer(r, 0, xh, z, y, d)},
        )

    def gather_wait(a, r, h, q):
        where = xh if h == 0 else 1 - xh
        spot = ag.at[a, r, (own[r] + q) % 4, pl.ds(where * 128, 128)]
        back = (4 - q) % 4
        remote(spot, spot, gs.at[a, r, h, back], gr.at[a, r, h, back], partner).wait_recv()

    def landing(a, r, sender, group):
        row = (sender * 4 + group) if r == 0 else (group * 4 + sender)
        return xb.at[a, r, pl.ds(row * 80, 80)]

    def spread_copy(a, r, q, d):
        group = (own[r] + q) % 4
        me = own[1 - r]
        return remote(
            sb.at[a, r, (me + d) % 4, q], landing(a, r, me, group),
            us.at[a, r, q, d], ur.at[a, r, q, d],
            {"expert": peer(r, 1, xh, z, y, d)},
        )

    def keep_copy(a, r, q):
        group = (own[r] + q) % 4
        me = own[1 - r]
        return pltpu.make_async_copy(sb.at[a, r, me, q], landing(a, r, me, group), lo.at[a, r, q])

    metas = (m1, m2)

    def meta_copy(r, dx, d):
        to_x = (xh + dx) % 2
        to = (own[r] + d) % 4
        where = number(to_x, z, to) if r == 0 else number(to_x, to, y)
        return remote(
            metas[r].at[to_x, to], mr.at[r, own[r], xh], ms.at[r, dx, d], mrs.at[r, dx, d],
            {"expert": where},
        )

    for r in range(2):
        x_copy(0, r).start()
        own_copy(0, r).start()
    for d in ORDER:
        for r in range(2):
            gather_copy(0, r, 0, d).start()
    for r in range(2):
        x_copy(1, r).start()
        own_copy(1, r).start()
    for load in loads:
        load.start()
    pairs = [(dx, d) for dx in range(2) for d in range(4) if dx or d]
    metadata(rt, gt, m1, m2)
    for r in range(2):
        mr[r, own[r], xh] = metas[r][xh, own[r]]
    for r in range(2):
        for dx, d in pairs:
            meta_copy(r, dx, d).start()

    def pass_on(a):
        for r in range(2):
            own_copy(a, r).wait()
            spot = ag.at[a, r, own[r], pl.ds((1 - xh) * 128, 128)]
            remote(spot, spot, xs.at[a, r], xr.at[a, r], partner).wait_recv()
            for d in ORDER:
                gather_copy(a, r, 1, d).start()

    pass_on(0)
    for d in ORDER:
        for r in range(2):
            gather_copy(1, r, 0, d).start()
    for r in range(2):
        for dx, d in pairs:
            meta_copy(r, dx, d).wait()

    def spread(a):
        def body(i, carry):
            q = turn(i)
            for r in range(2):
                group = (own[r] + q) % 4

                @pl.when(i > 0)
                def _():
                    gather_wait(a, r, 0, q)
                    gather_wait(a, r, 1, q)

                hit, share = selection(mr, r, group)
                hit = hit.astype(BF)
                for c in range(2):
                    part = pl.ds(c * (half // 2), half // 2)
                    rows = jnp.dot(hit, ag[a, r, group, :, part], preferred_element_type=F32)
                    if a == 1:
                        rows = rows * jnp.sum(share, axis=1, keepdims=True)
                    rows = rows.astype(BF)
                    for e in range(4):
                        sb[a, r, e, q, :, part] = rows[e * 80 : e * 80 + 80]
                for d in ORDER:
                    spread_copy(a, r, q, d).start()
                keep_copy(a, r, q).start()
            return carry

        lax.fori_loop(0, 4, body, 0)

    spread(0)
    pass_on(1)
    spread(1)
    results = (xo, yo)

    def arrive(a):
        for r in range(2):
            for q in range(4):
                keep_copy(a, r, q).wait()
                for d in ORDER:
                    spread_copy(a, r, q, d).wait()
            pltpu.make_async_copy(xb.at[a, r], results[a].at[r], os_.at[a, r]).start()

    arrive(0)
    for load in loads:
        load.wait()

    def stores(t):
        part = pl.ds(t * 320, 320)
        found = [
            pltpu.make_async_copy(gus.at[part], guo.at[part], fo.at[t, 0]),
            pltpu.make_async_copy(acs.at[part], aco.at[part], fo.at[t, 1]),
        ]
        for r in range(2):
            found.append(pltpu.make_async_copy(prs.at[r, part], po.at[r, part], fo.at[t, 2 + r]))
        return found

    def forward(t, carry):
        part = pl.ds(t * 320, 320)
        both = jnp.dot(xb[0, 0, part], wgu[pl.ds(0, half)], preferred_element_type=F32)
        both = both + jnp.dot(xb[0, 1, part], wgu[pl.ds(half, half)], preferred_element_type=F32)
        both = both * scale_in
        gus[part] = both
        gate = both[:, :hidden]
        act = (gate * jax.nn.sigmoid(gate) * both[:, hidden:]).astype(BF)
        acs[part] = act
        for r in range(2):
            made = jnp.dot(act, wdn[:, pl.ds(r * half, half)], preferred_element_type=F32)
            prs[r, part] = (made * scale_hidden).astype(BF)
        for s in stores(t):
            s.start()
        return carry

    lax.fori_loop(0, 4, forward, 0)
    arrive(1)
    mo[...] = mr[...]
    for t in range(4):
        for s in stores(t):
            s.wait()
    for a in range(2):
        for r in range(2):
            x_copy(a, r).wait_send()
            for h in range(2):
                for d in ORDER:
                    gather_copy(a, r, h, d).wait_send()
            pltpu.make_async_copy(xb.at[a, r], results[a].at[r], os_.at[a, r]).wait()


def dispatch(tokens, cotangent, rt, gt, wg, wu, wd):
    rows, width = tokens.shape
    half = width // 2
    hidden = wd.shape[0]
    dma = pltpu.SemaphoreType.DMA
    anywhere = pl.BlockSpec(memory_space=pl.ANY)
    vmem = pl.BlockSpec(memory_space=pltpu.VMEM)
    slots = 32 * CAP
    halves = jax.ShapeDtypeStruct((2, slots, half), BF)
    return pl.pallas_call(
        dispatch_kernel,
        out_shape=(
            halves, halves, halves,
            jax.ShapeDtypeStruct((slots, 2 * hidden), F32),
            jax.ShapeDtypeStruct((slots, hidden), BF),
            jax.ShapeDtypeStruct((2, 4, 2, 8, 128), F32),
        ),
        in_specs=[anywhere, anywhere, vmem, vmem, anywhere, anywhere, anywhere],
        out_specs=(*[anywhere] * 5, vmem),
        scratch_shapes=[
            pltpu.VMEM((2, 2, 4, 256, half), BF),
            pltpu.VMEM((2, 2, 4, 4, 80, half), BF),
            pltpu.VMEM((2, 2, slots, half), BF),
            pltpu.VMEM((2, 4, 2, 8, 128), F32),
            pltpu.VMEM((2, 4, 8, 128), F32),
            pltpu.VMEM((2, 4, 8, 128), F32),
            pltpu.VMEM((width, 2 * hidden), BF),
            pltpu.VMEM((hidden, width), BF),
            pltpu.VMEM((slots, 2 * hidden), F32),
            pltpu.VMEM((slots, hidden), BF),
            pltpu.VMEM((2, slots, half), BF),
            dma((2, 2, 4)), dma((2, 2, 4)),
            dma((2, 2)), dma((2, 2)),
            dma((2, 2, 2, 4)), dma((2, 2, 2, 4)),
            dma((2, 2, 4, 4)), dma((2, 2, 4, 4)),
            dma((2, 2)), dma((2, 2, 4)), dma((2, 2)),
            dma((3,)), dma((4, 4)),
        ],
        compiler_params=pltpu.CompilerParams(
            collective_id=0, has_side_effects=True, vmem_limit_bytes=60 * 2**20
        ),
        name="dispatch",
    )(tokens, cotangent, rt, gt, wg, wu, wd)


def combine_kernel(
    xi, yi, pr, gui, aci, mr, wg, wu, wd, mg, mu, md,
    out, tg, lgu_o, ld_o, mgu_o, md_o, bgu, bd,
    xv, yv, gup, acv, grads, wgu, wdn, mgu, mdn, lgu, ldn,
    rb, qs, qr, xsend, xrecv, mine, kept,
    cs, cr, ls, ps, pt, xs, xr, ws, wr, wl, go,
):
    xh, z, y = place()
    rep = lax.axis_index("replica")
    half = rb.shape[-1]
    hidden = wd.shape[0]
    scale_in = (2 * half) ** (-0.5)
    scale_hidden = hidden ** (-0.5)
    low, high = pl.ds(0, hidden), pl.ds(hidden, hidden)
    copies = [
        (wd, wdn), (yi, yv), (gui, gup), (xi, xv), (wg, wgu.at[:, low]), (wu, wgu.at[:, high]),
        (mg, mgu.at[:, low]), (mu, mgu.at[:, high]), (aci, acv), (md, mdn),
    ]
    loads = [pltpu.make_async_copy(s, d, wl.at[i]) for i, (s, d) in enumerate(copies)]
    for load in loads:
        load.start()
    own = (y, z)
    partner = {"expert": number(1 - xh, z, y)}
    core_mate = {"replica": rep + 1 - 2 * (rep % 2)}
    far_mate = {"replica": (rep + 2) % 4}
    others = [partner, core_mate, far_mate]
    for d in ORDER:
        others.append({"expert": number(xh, z, (y + d) % 4)})
        others.append({"expert": number(xh, (z + d) % 4, y)})
    greet(others)
    source = (pr, xv)
    results = (out, tg)

    def block(a, r, e, group):
        row = (e * 4 + group) if r == 0 else (group * 4 + e)
        return source[a].at[r, pl.ds(row * 80, 80)]

    def send_copy(a, r, q, d):
        group = (own[r] + q) % 4
        me = own[1 - r]
        return remote(
            block(a, r, (me + d) % 4, group), rb.at[a, r, group, me],
            cs.at[a, r, q, d], cr.at[a, r, q, d],
            {"expert": peer(r, 1, xh, z, y, d)},
        )

    def keep_copy(a, r, q):
        group = (own[r] + q) % 4
        me = own[1 - r]
        return pltpu.make_async_copy(block(a, r, me, group), rb.at[a, r, group, me], ls.at[a, r, q])

    def part_copy(a, r, q):
        return remote(
            qs.at[a, r, q - 1], qr.at[a, r, q - 1], ps.at[a, r, q], pt.at[a, r, q],
            {"expert": peer(r, 0, xh, z, y, q)},
        )

    def x_copy(a, r):
        return remote(xsend.at[a, r], xrecv.at[a, r], xs.at[a, r], xr.at[a, r], partner)

    def send_rows(a):
        for q in (1, 3, 2, 0):
            for r in range(2):
                keep_copy(a, r, q).start()
            for d in ORDER:
                for r in range(2):
                    send_copy(a, r, q, d).start()

    def in_tile(t):
        rows = pl.ds(t * 256, 256)
        src = lgu.at[rows]
        return [
            remote(src, bgu.at[1, rows], ws.at[1, t], wr.at[1, t], far_mate),
            remote(src, bgu.at[0, rows], ws.at[0, t], wr.at[0, t], core_mate),
        ]

    def down_tile(c):
        cols = pl.ds(c * 512, 512)
        src = ldn.at[:, cols]
        return [
            remote(src, bd.at[1, :, cols], ws.at[1, 8 + c], wr.at[1, 8 + c], far_mate),
            remote(src, bd.at[0, :, cols], ws.at[0, 8 + c], wr.at[0, 8 + c], core_mate),
        ]

    send_rows(0)
    for load in loads[:3]:
        load.wait()

    def hidden_grads(t, carry):
        part = pl.ds(t * 320, 320)
        inner = (((1,), (1,)), ((), ()))
        grad_act = lax.dot_general(
            yv[0, part], wdn[:, pl.ds(0, half)], inner, preferred_element_type=F32
        )
        grad_act = grad_act + lax.dot_general(
            yv[1, part], wdn[:, pl.ds(half, half)], inner, preferred_element_type=F32
        )
        grad_act = grad_act * scale_hidden
        gate = gup[part, low]
        up = gup[part, high]
        sig = jax.nn.sigmoid(gate)
        grads[part, low] = (grad_act * up * sig * (1.0 + gate * (1.0 - sig))).astype(BF)
        grads[part, high] = (grad_act * gate * sig).astype(BF)
        return carry

    lax.fori_loop(0, 4, hidden_grads, 0)
    for load in loads[3:8]:
        load.wait()
    outer = (((0,), (0,)), ((), ()))

    def in_grads(t, carry):
        rows = pl.ds(t * 256, 256)
        cols = pl.ds((t % 4) * 256, 256)
        grad = lax.dot_general(
            xv[t // 4, :, cols], grads[...], outer, preferred_element_type=F32
        ) * scale_in
        moment = momentum_beta * mgu[rows].astype(F32) + grad
        mgu[rows] = moment.astype(BF)
        lgu[rows] = (wgu[rows].astype(F32) - learn_rate * moment).astype(BF)
        for s in in_tile(t):
            s.start()
        return carry

    lax.fori_loop(0, 8, in_grads, 0)
    for load in loads[8:]:
        load.wait()

    def down_grads(c, carry):
        cols = pl.ds((c % 2) * 512, 512)
        where = pl.ds(c * 512, 512)
        grad = lax.dot_general(
            acv[...], yv[c // 2, :, cols], outer, preferred_element_type=F32
        ) * scale_hidden
        moment = momentum_beta * mdn[:, where].astype(F32) + grad
        mdn[:, where] = moment.astype(BF)
        ldn[:, where] = (wdn[:, where].astype(F32) - learn_rate * moment).astype(BF)
        for s in down_tile(c):
            s.start()
        return carry

    lax.fori_loop(0, 4, down_grads, 0)

    def back_rows(t, carry):
        part = pl.ds(t * 320, 320)
        inner = (((1,), (1,)), ((), ()))
        for r in range(2):
            back = lax.dot_general(
                grads[part], wgu[pl.ds(r * half, half)], inner, preferred_element_type=F32
            )
            xv[r, part] = (back * scale_in).astype(BF)
        return carry

    lax.fori_loop(0, 4, back_rows, 0)
    send_rows(1)
    moments = [
        pltpu.make_async_copy(s, d, go.at[i])
        for i, (s, d) in enumerate(((mgu, mgu_o), (mdn, md_o), (lgu, lgu_o), (ldn, ld_o)))
    ]
    for m in moments:
        m.start()

    def reduce(a):
        def body(i, carry):
            q = turn((i + 1) % 4)
            for r in range(2):
                group = (own[r] + q) % 4
                keep_copy(a, r, q).wait()
                for d in ORDER:
                    send_copy(a, r, q, d).wait_recv()
                hit, share = selection(mr, r, group)
                pick = (share if a == 0 else hit).astype(BF)
                for c in range(2):
                    part = pl.ds(c * (half // 2), half // 2)
                    rows = jnp.concatenate([rb[a, r, group, e, :, part] for e in range(4)], axis=0)
                    total = lax.dot_general(pick, rows, outer, preferred_element_type=F32)

                    @pl.when(i < 3)
                    def _():
                        qs[a, r, (q + 3) % 4, :, part] = total.astype(BF)

                    @pl.when(i == 3)
                    def _():
                        mine[r, :, part] = total

                @pl.when(i < 3)
                def _():
                    part_copy(a, r, q).start()
            return carry

        lax.fori_loop(0, 4, body, 0)
        there = pl.ds((1 - xh) * 128, 128)
        here = pl.ds(xh * 128, 128)
        for r in range(2):
            for q in ORDER:
                part_copy(a, r, q).wait_recv()
            away = mine[r, there]
            stay = mine[r, here]
            for q in ORDER:
                away = away + qr[a, r, q - 1, there].astype(F32)
                stay = stay + qr[a, r, q - 1, here].astype(F32)
            xsend[a, r] = away.astype(BF)
            x_copy(a, r).start()
            kept[a, r] = stay

    reduce(0)
    reduce(1)
    for a in range(2):
        for r in range(2):
            x_copy(a, r).wait_recv()
            total = kept[a, r] + xrecv[a, r].astype(F32)
            results[a][:, pl.ds(r * half, half)] = total.astype(BF)
    for a in range(2):
        for r in range(2):
            x_copy(a, r).wait_send()
            for q in range(4):
                for d in ORDER:
                    send_copy(a, r, q, d).wait_send()
            for q in ORDER:
                part_copy(a, r, q).wait_send()
    for t in range(8):
        for s in in_tile(t):
            s.wait()
    for c in range(4):
        for s in down_tile(c):
            s.wait()
    for m in moments:
        m.wait()


def combine(xi, yi, pr, gui, aci, mr, wg, wu, wd, mg, mu, md):
    half = xi.shape[2]
    width = 2 * half
    slots = xi.shape[1]
    hidden = wd.shape[0]
    dma = pltpu.SemaphoreType.DMA
    anywhere = pl.BlockSpec(memory_space=pl.ANY)
    vmem = pl.BlockSpec(memory_space=pltpu.VMEM)
    tokens = jax.ShapeDtypeStruct((128, width), BF)
    inward = jax.ShapeDtypeStruct((width, 2 * hidden), BF)
    down = jax.ShapeDtypeStruct((hidden, width), BF)
    return pl.pallas_call(
        combine_kernel,
        out_shape=(
            tokens, tokens, inward, down, inward, down,
            jax.ShapeDtypeStruct((2, width, 2 * hidden), BF),
            jax.ShapeDtypeStruct((2, hidden, width), BF),
        ),
        in_specs=[*[anywhere] * 5, vmem, *[anywhere] * 6],
        out_specs=(vmem, vmem, *[anywhere] * 6),
        scratch_shapes=[
            pltpu.VMEM((2, slots, half), BF),
            pltpu.VMEM((2, slots, half), BF),
            pltpu.VMEM((slots, 2 * hidden), F32),
            pltpu.VMEM((slots, hidden), BF),
            pltpu.VMEM((slots, 2 * hidden), BF),
            pltpu.VMEM((width, 2 * hidden), BF),
            pltpu.VMEM((hidden, width), BF),
            pltpu.VMEM((width, 2 * hidden), BF),
            pltpu.VMEM((hidden, width), BF),
            pltpu.VMEM((width, 2 * hidden), BF),
            pltpu.VMEM((hidden, width), BF),
            pltpu.VMEM((2, 2, 4, 4, 80, half), BF),
            pltpu.VMEM((2, 2, 3, 256, half), BF),
            pltpu.VMEM((2, 2, 3, 256, half), BF),
            pltpu.VMEM((2, 2, 128, half), BF),
            pltpu.VMEM((2, 2, 128, half), BF),
            pltpu.VMEM((2, 256, half), F32),
            pltpu.VMEM((2, 2, 128, half), F32),
            dma((2, 2, 4, 4)), dma((2, 2, 4, 4)),
            dma((2, 2, 4)),
            dma((2, 2, 4)), dma((2, 2, 4)),
            dma((2, 2)), dma((2, 2)),
            dma((2, 12)), dma((2, 12)),
            dma((10,)), dma((4,)),
        ],
        compiler_params=pltpu.CompilerParams(
            collective_id=1, has_side_effects=True, vmem_limit_bytes=63 * 2**20
        ),
        name="combine",
    )(xi, yi, pr, gui, aci, mr, wg, wu, wd, mg, mu, md)


def finish_kernel(
    bit, lgu, bgu, mgu, ld, bd, md, out, tg,
    ng, nu, nd, mgo, muo, mdo, oo, to,
):
    hidden = ng.shape[1]
    inward = ((lgu[...].astype(F32) + bgu[0].astype(F32)) * 0.5).astype(BF)
    ng[...] = inward[:, :hidden]
    nu[...] = inward[:, hidden:]
    nd[...] = ((ld[...].astype(F32) + bd[0].astype(F32)) * 0.5).astype(BF)
    mgo[...] = mgu[:, :hidden]
    muo[...] = mgu[:, hidden:]
    mdo[...] = md[...]
    oo[...] = out[...]
    to[...] = tg[...]


def finish(bit, lgu, bgu, mgu, ld, bd, md, out, tg):
    width, both = lgu.shape
    hidden = both // 2
    steps = 4
    tile = width // steps
    rows = pl.BlockSpec((tile, both), lambda i, b: (i, 0))
    half_rows = pl.BlockSpec((tile, hidden), lambda i, b: (i, 0))
    cols = pl.BlockSpec((hidden, tile), lambda i, b: (0, i))
    toks = pl.BlockSpec((128, tile), lambda i, b: (0, i))
    shape = jax.ShapeDtypeStruct
    return pl.pallas_call(
        finish_kernel,
        out_shape=(
            shape((width, hidden), BF), shape((width, hidden), BF), shape((hidden, width), BF),
            shape((width, hidden), BF), shape((width, hidden), BF), shape((hidden, width), BF),
            shape((128, width), BF), shape((128, width), BF),
        ),
        grid_spec=pltpu.PrefetchScalarGridSpec(
            num_scalar_prefetch=1,
            grid=(steps,),
            in_specs=[
                rows, pl.BlockSpec((1, tile, both), lambda i, b: (b[0], i, 0)), rows,
                cols, pl.BlockSpec((1, hidden, tile), lambda i, b: (b[0], 0, i)), cols,
                toks, toks,
            ],
            out_specs=(half_rows, half_rows, cols, half_rows, half_rows, cols, toks, toks),
        ),
        compiler_params=pltpu.CompilerParams(vmem_limit_bytes=62 * 2**20),
        name="finish",
    )(bit, lgu, bgu, mgu, ld, bd, md, out, tg)


def per_device(
    tokens, routing, gate_scores, cotangent,
    w_gate, w_up, w_down, mom_gate, mom_up, mom_down, gossip_round,
):
    wg, wu, wd = w_gate[0, 0], w_up[0, 0], w_down[0, 0]
    xi, yi, pr, gui, aci, meta = dispatch(
        tokens, cotangent, routing.T, gate_scores.T, wg, wu, wd
    )
    out, tg, lgu, ld, mgu, md, bgu, bd = combine(
        xi, yi, pr, gui, aci, meta, wg, wu, wd, mom_gate[0, 0], mom_up[0, 0], mom_down[0, 0]
    )
    ng, nu, nd, mg, mu, mdn, layer_out, token_grad = finish(
        gossip_round % 2, lgu, bgu, mgu, ld, bd, md, out, tg
    )
    return (
        layer_out, token_grad, ng[None, None], nu[None, None], nd[None, None],
        mg[None, None], mu[None, None], mdn[None, None],
    )


def solution(mesh):
    flat = P(("replica", "expert"), None)
    stacked = P("replica", "expert", None, None)
    return jax.shard_map(
        per_device,
        mesh=mesh,
        in_specs=(flat,) * 4 + (stacked,) * 6 + (P("expert"),),
        out_specs=(flat,) * 2 + (stacked,) * 6,
        check_vma=False,
    )
```

```python
import jax
import jax.numpy as jnp
from jax import lax
from jax.experimental import pallas as pl
from jax.experimental.pallas import tpu as pltpu
from jax.sharding import PartitionSpec as P

momentum_beta = 0.9
learn_rate = 0.1
MESH = pl.DeviceIdType.MESH
CAP = 40
BF = jnp.bfloat16
F32 = jnp.float32
ORDER = (1, 3, 2)
NEAR = (1, 3)


def place():
    e = lax.axis_index("expert")
    return e // 16, (e // 4) % 4, e % 4


def number(xh, z, y):
    return xh * 16 + z * 4 + y


def peer(route, stage, xh, z, y, d):
    if (route == 0) == (stage == 0):
        return number(xh, z, (y + d) % 4)
    return number(xh, (z + d) % 4, y)


def greet(ids):
    barrier = pltpu.get_barrier_semaphore()
    for where in ids:
        pl.semaphore_signal(barrier, inc=1, device_id=where, device_id_type=MESH)
    pl.semaphore_wait(barrier, len(ids))


def remote(src, dst, ss, rs, where):
    return pltpu.make_async_remote_copy(
        src_ref=src, dst_ref=dst, send_sem=ss, recv_sem=rs, device_id=where, device_id_type=MESH
    )


def turn(i):
    return i + i // 2 - 2 * (i // 3)


def selection(meta, route, group):
    width = 128
    rows = lax.broadcasted_iota(jnp.int32, (2 * CAP, width), 0).astype(F32)
    first = meta[route, group, 0]
    second = meta[route, group, 1]
    hits, shares = [], []
    for e in range(4):
        hit = jnp.concatenate(
            [rows == first[e : e + 1, :], rows == second[e : e + 1, :] + float(CAP)], axis=1
        )
        share = jnp.concatenate([first[4 + e : 5 + e, :], second[4 + e : 5 + e, :]], axis=1)
        hits.append(hit)
        shares.append(jnp.where(hit, share, 0.0))
    hit = jnp.concatenate([jnp.where(h, 1.0, 0.0) for h in hits], axis=0)
    return hit, jnp.concatenate(shares, axis=0)


def metadata(rt, gt, m1, m2):
    share = gt[...] / jnp.sum(gt[...], axis=0, keepdims=True)
    names = lax.broadcasted_iota(jnp.int32, (32, 128), 0)
    member = jnp.zeros((32, 128), F32)
    shares = jnp.zeros((32, 128), F32)
    for k in range(8):
        same = rt[k : k + 1, :] == names
        member = member + jnp.where(same, 1.0, 0.0)
        shares = shares + jnp.where(same, share[k : k + 1, :], 0.0)
    earlier_token = lax.broadcasted_iota(jnp.int32, (128, 128), 0)
    later_token = lax.broadcasted_iota(jnp.int32, (128, 128), 1)
    before = jnp.where(earlier_token < later_token, 1.0, 0.0).astype(BF)
    earlier = jnp.dot(member.astype(BF), before, preferred_element_type=F32)
    slots = jnp.where(member > 0.0, earlier, -1000.0)
    for xh in range(2):
        for i in range(4):
            for k in range(4):
                e1 = xh * 16 + k * 4 + i
                e2 = xh * 16 + i * 4 + k
                m1[xh, i, k : k + 1, :] = slots[e1 : e1 + 1]
                m1[xh, i, 4 + k : 5 + k, :] = shares[e1 : e1 + 1]
                m2[xh, i, k : k + 1, :] = slots[e2 : e2 + 1]
                m2[xh, i, 4 + k : 5 + k, :] = shares[e2 : e2 + 1]


def dispatch_kernel(
    tok, cot, rt, gt, wg, wu, wd,
    xo, yo, po, aco, gro, mo,
    ag, sb, xb, mr, m1, m2, wgu, wdn, gus, acs, prs, gas, grs,
    ms, mrs, xs, xr, gs, gr, us, ur, ls, lo, os_, wl, fo, hs, hr, go, ks, kr,
):
    xh, z, y = place()
    half = ag.shape[-1]
    hidden = wd.shape[0]
    scale_in = (2 * half) ** (-0.5)
    scale_hidden = hidden ** (-0.5)
    loads = [
        pltpu.make_async_copy(wg, wgu.at[:, pl.ds(0, hidden)], wl.at[0]),
        pltpu.make_async_copy(wu, wgu.at[:, pl.ds(hidden, hidden)], wl.at[1]),
        pltpu.make_async_copy(wd, wdn, wl.at[2]),
    ]
    others = []
    for dx in range(2):
        for d in range(4):
            if dx or d:
                others.append({"expert": number((xh + dx) % 2, z, (y + d) % 4)})
            if d:
                others.append({"expert": number((xh + dx) % 2, (z + d) % 4, y)})
    greet(others)
    own = (y, z)
    source = (tok, cot)
    partner = {"expert": number(1 - xh, z, y)}

    def cols(a, r):
        return source[a].at[:, pl.ds(r * half, half)]

    def x_copy(a, r):
        spot = ag.at[a, r, own[r], pl.ds(xh * 128, 128)]
        return remote(cols(a, r), spot, xs.at[a, r], xr.at[a, r], partner)

    def cross_copy(r, q):
        spot = ag.at[1, r, (own[r] + q) % 4, pl.ds(xh * 128, 128)]
        return remote(spot, spot, ks.at[r, q], kr.at[r, q], partner)

    def cross_wait(r, q):
        spot = ag.at[1, r, (own[r] + q) % 4, pl.ds((1 - xh) * 128, 128)]
        remote(spot, spot, ks.at[r, q], kr.at[r, q], partner).wait_recv()

    def own_copy(a, r):
        return pltpu.make_async_copy(
            cols(a, r), ag.at[a, r, own[r], pl.ds(xh * 128, 128)], ls.at[a, r]
        )

    def gather_copy(a, r, h, d):
        where = xh if h == 0 else 1 - xh
        spot = ag.at[a, r, own[r], pl.ds(where * 128, 128)]
        src = cols(a, r) if h == 0 else spot
        return remote(
            src, spot, gs.at[a, r, h, d], gr.at[a, r, h, d],
            {"expert": peer(r, 0, xh, z, y, d)},
        )

    def gather_wait(a, r, h, q):
        where = xh if h == 0 else 1 - xh
        spot = ag.at[a, r, (own[r] + q) % 4, pl.ds(where * 128, 128)]
        back = (4 - q) % 4
        remote(spot, spot, gs.at[a, r, h, back], gr.at[a, r, h, back], partner).wait_recv()

    def relay_copy(a, r, h, side):
        where = xh if h == 0 else 1 - xh
        came, to = ((own[r] + 3) % 4, 1) if side == 0 else ((own[r] + 1) % 4, 3)
        spot = ag.at[a, r, came, pl.ds(where * 128 + side * 64, 64)]
        return remote(
            spot, spot, hs.at[a, r, h, side], hr.at[a, r, h, side],
            {"expert": peer(r, 0, xh, z, y, to)},
        )

    def relay_wait(a, r, h, side):
        where = xh if h == 0 else 1 - xh
        spot = ag.at[a, r, (own[r] + 2) % 4, pl.ds(where * 128 + side * 64, 64)]
        remote(spot, spot, hs.at[a, r, h, side], hr.at[a, r, h, side], partner).wait_recv()

    def relay(a, h):
        for r in range(2):
            gather_wait(a, r, h, 3)
            relay_copy(a, r, h, 0).start()
            gather_wait(a, r, h, 1)
            relay_copy(a, r, h, 1).start()

    def landing(a, r, sender, group):
        row = (sender * 4 + group) if r == 0 else (group * 4 + sender)
        return xb.at[a, r, pl.ds(row * 80, 80)]

    def spread_copy(a, r, q, d):
        group = (own[r] + q) % 4
        me = own[1 - r]
        return remote(
            sb.at[a, r, (me + d) % 4, q], landing(a, r, me, group),
            us.at[a, r, q, d], ur.at[a, r, q, d],
            {"expert": peer(r, 1, xh, z, y, d)},
        )

    def keep_copy(a, r, q):
        group = (own[r] + q) % 4
        me = own[1 - r]
        return pltpu.make_async_copy(sb.at[a, r, me, q], landing(a, r, me, group), lo.at[a, r, q])

    metas = (m1, m2)

    def meta_copy(r, dx, d):
        to_x = (xh + dx) % 2
        to = (own[r] + d) % 4
        where = number(to_x, z, to) if r == 0 else number(to_x, to, y)
        return remote(
            metas[r].at[to_x, to], mr.at[r, own[r], xh], ms.at[r, dx, d], mrs.at[r, dx, d],
            {"expert": where},
        )

    for r in range(2):
        x_copy(0, r).start()
        own_copy(0, r).start()
    for d in NEAR:
        for r in range(2):
            gather_copy(0, r, 0, d).start()
    for r in range(2):
        x_copy(1, r).start()
        own_copy(1, r).start()
    for d in NEAR:
        for r in range(2):
            gather_copy(1, r, 0, d).start()
    for load in loads:
        load.start()
    pairs = [(dx, d) for dx in range(2) for d in range(4) if dx or d]
    metadata(rt, gt, m1, m2)
    for r in range(2):
        mr[r, own[r], xh] = metas[r][xh, own[r]]
    for r in range(2):
        for dx, d in pairs:
            meta_copy(r, dx, d).start()

    def pass_on(a):
        for r in range(2):
            own_copy(a, r).wait()
            spot = ag.at[a, r, own[r], pl.ds((1 - xh) * 128, 128)]
            remote(spot, spot, xs.at[a, r], xr.at[a, r], partner).wait_recv()
            if a == 0:
                for d in NEAR:
                    gather_copy(a, r, 1, d).start()

    relay(0, 0)
    pass_on(0)
    relay(1, 0)
    for q in NEAR:
        for r in range(2):
            cross_copy(r, q).start()
    for r in range(2):
        for dx, d in pairs:
            meta_copy(r, dx, d).wait()

    def spread(a):
        def body(i, carry):
            q = turn(i)

            if a == 0:

                @pl.when(i == 1)
                def _():
                    relay(0, 1)

                @pl.when(i == 2)
                def _():
                    for r in range(2):
                        for side in range(2):
                            relay_wait(1, r, 0, side)
                        cross_copy(r, 2).start()

            for r in range(2):
                group = (own[r] + q) % 4

                if a == 0:

                    @pl.when(i == 3)
                    def _():
                        for h in range(2):
                            for side in range(2):
                                relay_wait(0, r, h, side)

                else:

                    @pl.when(i > 0)
                    def _():
                        cross_wait(r, q)

                hit, share = selection(mr, r, group)
                hit = hit.astype(BF)
                for c in range(2):
                    part = pl.ds(c * (half // 2), half // 2)
                    rows = jnp.dot(hit, ag[a, r, group, :, part], preferred_element_type=F32)
                    if a == 1:
                        rows = rows * jnp.sum(share, axis=1, keepdims=True)
                    rows = rows.astype(BF)
                    for e in range(4):
                        sb[a, r, e, q, :, part] = rows[e * 80 : e * 80 + 80]
                for d in ORDER:
                    spread_copy(a, r, q, d).start()
                keep_copy(a, r, q).start()
            return carry

        lax.fori_loop(0, 4, body, 0)

    spread(0)
    pass_on(1)
    spread(1)
    results = (xo, yo)

    def landed(a, r, q):
        keep_copy(a, r, q).wait()
        for d in ORDER:
            spread_copy(a, r, q, d).wait()

    def leave(a, r):
        pltpu.make_async_copy(xb.at[a, r], results[a].at[r], os_.at[a, r]).start()

    for r in range(2):
        for q in range(4):
            landed(0, r, q)
        leave(0, r)
    for load in loads:
        load.wait()

    def stores(t):
        part = pl.ds(t * 320, 320)
        found = [
            pltpu.make_async_copy(acs.at[part], aco.at[part], fo.at[t, 0]),
        ]
        for r in range(2):
            found.append(pltpu.make_async_copy(prs.at[r, part], po.at[r, part], fo.at[t, 1 + r]))
        return found

    def forward(t, carry):
        part = pl.ds(t * 320, 320)
        both = jnp.dot(xb[0, 0, part], wgu[pl.ds(0, half)], preferred_element_type=F32)
        both = both + jnp.dot(xb[0, 1, part], wgu[pl.ds(half, half)], preferred_element_type=F32)
        both = both * scale_in
        gus[part] = both
        gate = both[:, :hidden]
        act = (gate * jax.nn.sigmoid(gate) * both[:, hidden:]).astype(BF)
        acs[part] = act
        for r in range(2):
            made = jnp.dot(act, wdn[:, pl.ds(r * half, half)], preferred_element_type=F32)
            prs[r, part] = (made * scale_hidden).astype(BF)
        for s in stores(t):
            s.start()
        return carry

    lax.fori_loop(0, 4, forward, 0)
    gas[...] = jnp.zeros_like(gas)
    inner = (((1,), (1,)), ((), ()))

    def grad_part(i, carry):
        q = turn(i)
        landed(1, 0, q)
        spots = [pl.ds((k * 4 + (y + q) % 4) * 80, 80) for k in range(4)]
        rows = jnp.concatenate([xb[1, 0, s] for s in spots], axis=0)
        more = lax.dot_general(rows, wdn[:, pl.ds(0, half)], inner, preferred_element_type=F32)
        for k, s in enumerate(spots):
            gas[s] += more[k * 80 : k * 80 + 80]
        landed(1, 1, q)
        part = pl.ds(((z + q) % 4) * 320, 320)
        gas[part] += lax.dot_general(
            xb[1, 1, part], wdn[:, pl.ds(half, half)], inner, preferred_element_type=F32
        )
        return carry

    lax.fori_loop(0, 4, grad_part, 0)
    for r in range(2):
        leave(1, r)
    mo[...] = mr[...]

    def grad_store(t):
        part = pl.ds(t * 160, 160)
        return pltpu.make_async_copy(grs.at[part], gro.at[part], go.at[t])

    def hidden_grads(t, carry):
        part = pl.ds(t * 160, 160)
        grad_act = gas[part] * scale_hidden
        gate = gus[part, pl.ds(0, hidden)]
        up = gus[part, pl.ds(hidden, hidden)]
        sig = jax.nn.sigmoid(gate)
        grs[part, pl.ds(0, hidden)] = (
            grad_act * up * sig * (1.0 + gate * (1.0 - sig))
        ).astype(BF)
        grs[part, pl.ds(hidden, hidden)] = (grad_act * gate * sig).astype(BF)
        grad_store(t).start()
        return carry

    lax.fori_loop(0, 8, hidden_grads, 0)
    for t in range(8):
        grad_store(t).wait()
    for r in range(2):
        for q in ORDER:
            cross_copy(r, q).wait_send()
    for t in range(4):
        for s in stores(t):
            s.wait()
    for a in range(2):
        for r in range(2):
            x_copy(a, r).wait_send()
            for h in range(2 - a):
                for d in NEAR:
                    gather_copy(a, r, h, d).wait_send()
                for side in range(2):
                    relay_copy(a, r, h, side).wait_send()
            pltpu.make_async_copy(xb.at[a, r], results[a].at[r], os_.at[a, r]).wait()


def dispatch(tokens, cotangent, rt, gt, wg, wu, wd):
    rows, width = tokens.shape
    half = width // 2
    hidden = wd.shape[0]
    dma = pltpu.SemaphoreType.DMA
    anywhere = pl.BlockSpec(memory_space=pl.ANY)
    vmem = pl.BlockSpec(memory_space=pltpu.VMEM)
    slots = 32 * CAP
    halves = jax.ShapeDtypeStruct((2, slots, half), BF)
    return pl.pallas_call(
        dispatch_kernel,
        out_shape=(
            halves, halves, halves,
            jax.ShapeDtypeStruct((slots, hidden), BF),
            jax.ShapeDtypeStruct((slots, 2 * hidden), BF),
            jax.ShapeDtypeStruct((2, 4, 2, 8, 128), F32),
        ),
        in_specs=[anywhere, anywhere, vmem, vmem, anywhere, anywhere, anywhere],
        out_specs=(*[anywhere] * 5, vmem),
        scratch_shapes=[
            pltpu.VMEM((2, 2, 4, 256, half), BF),
            pltpu.VMEM((2, 2, 4, 4, 80, half), BF),
            pltpu.VMEM((2, 2, slots, half), BF),
            pltpu.VMEM((2, 4, 2, 8, 128), F32),
            pltpu.VMEM((2, 4, 8, 128), F32),
            pltpu.VMEM((2, 4, 8, 128), F32),
            pltpu.VMEM((width, 2 * hidden), BF),
            pltpu.VMEM((hidden, width), BF),
            pltpu.VMEM((slots, 2 * hidden), F32),
            pltpu.VMEM((slots, hidden), BF),
            pltpu.VMEM((2, slots, half), BF),
            pltpu.VMEM((slots, hidden), F32),
            pltpu.VMEM((slots, 2 * hidden), BF),
            dma((2, 2, 4)), dma((2, 2, 4)),
            dma((2, 2)), dma((2, 2)),
            dma((2, 2, 2, 4)), dma((2, 2, 2, 4)),
            dma((2, 2, 4, 4)), dma((2, 2, 4, 4)),
            dma((2, 2)), dma((2, 2, 4)), dma((2, 2)),
            dma((3,)), dma((4, 3)),
            dma((2, 2, 2, 2)), dma((2, 2, 2, 2)), dma((8,)),
            dma((2, 4)), dma((2, 4)),
        ],
        compiler_params=pltpu.CompilerParams(
            collective_id=0, has_side_effects=True, vmem_limit_bytes=60 * 2**20
        ),
        name="dispatch",
    )(tokens, cotangent, rt, gt, wg, wu, wd)


def combine_kernel(
    xi, yi, pr, aci, gri, mr, wg, wu, wd, mg, mu, md,
    out, tg, lgu_o, ld_o, mgu_o, md_o, bgu, bd,
    xv, yv, acv, grads, wgu, wdn, mgu, mdn, lgu, ldn,
    rb, qs, qr, xsend, xrecv, mine, kept,
    cs, cr, ls, ps, pt, xs, xr, ws, wr, wl, go,
):
    xh, z, y = place()
    rep = lax.axis_index("replica")
    half = rb.shape[-1]
    hidden = wd.shape[0]
    scale_in = (2 * half) ** (-0.5)
    scale_hidden = hidden ** (-0.5)
    low, high = pl.ds(0, hidden), pl.ds(hidden, hidden)
    copies = [(gri, grads)]
    for k in range(2):
        rows = pl.ds(k * half, half)
        copies.append((xi.at[k], xv.at[k]))
        for src, dst, cols in ((mg, mgu, low), (mu, mgu, high), (wg, wgu, low), (wu, wgu, high)):
            copies.append((src.at[rows], dst.at[rows, cols]))
    copies += [(aci, acv), (yi, yv), (md, mdn), (wd, wdn)]
    loads = [pltpu.make_async_copy(s, d, wl.at[i]) for i, (s, d) in enumerate(copies)]
    for load in loads:
        load.start()
    own = (y, z)
    partner = {"expert": number(1 - xh, z, y)}
    core_mate = {"replica": rep + 1 - 2 * (rep % 2)}
    far_mate = {"replica": (rep + 2) % 4}
    others = [partner, core_mate, far_mate]
    for d in ORDER:
        others.append({"expert": number(xh, z, (y + d) % 4)})
        others.append({"expert": number(xh, (z + d) % 4, y)})
    greet(others)
    source = (pr, xv)
    results = (out, tg)

    def block(a, r, e, group):
        row = (e * 4 + group) if r == 0 else (group * 4 + e)
        return source[a].at[r, pl.ds(row * 80, 80)]

    def send_copy(a, r, q, d):
        group = (own[r] + q) % 4
        me = own[1 - r]
        return remote(
            block(a, r, (me + d) % 4, group), rb.at[a, r, group, me],
            cs.at[a, r, q, d], cr.at[a, r, q, d],
            {"expert": peer(r, 1, xh, z, y, d)},
        )

    def keep_copy(a, r, q):
        group = (own[r] + q) % 4
        me = own[1 - r]
        return pltpu.make_async_copy(block(a, r, me, group), rb.at[a, r, group, me], ls.at[a, r, q])

    def part_copy(a, r, q):
        return remote(
            qs.at[a, r, q - 1], qr.at[a, r, q - 1], ps.at[a, r, q], pt.at[a, r, q],
            {"expert": peer(r, 0, xh, z, y, q)},
        )

    def x_copy(a, r):
        return remote(xsend.at[a, r], xrecv.at[a, r], xs.at[a, r], xr.at[a, r], partner)

    def send_rows(a):
        for q in (1, 3, 2, 0):
            for r in range(2):
                keep_copy(a, r, q).start()
            for d in ORDER:
                for r in range(2):
                    send_copy(a, r, q, d).start()

    def in_tile(t):
        rows = pl.ds(t * 256, 256)
        src = lgu.at[rows]
        return [
            remote(src, bgu.at[1, rows], ws.at[1, t], wr.at[1, t], far_mate),
            remote(src, bgu.at[0, rows], ws.at[0, t], wr.at[0, t], core_mate),
        ]

    def down_tile(c):
        cols = pl.ds(c * 512, 512)
        src = ldn.at[:, cols]
        return [
            remote(src, bd.at[1, :, cols], ws.at[1, 8 + c], wr.at[1, 8 + c], far_mate),
            remote(src, bd.at[0, :, cols], ws.at[0, 8 + c], wr.at[0, 8 + c], core_mate),
        ]

    send_rows(0)
    for load in loads[:6]:
        load.wait()
    outer = (((0,), (0,)), ((), ()))

    def in_grads(t, carry):
        @pl.when(t == 4)
        def _():
            for load in loads[6:11]:
                load.wait()

        rows = pl.ds(t * 256, 256)
        cols = pl.ds((t % 4) * 256, 256)
        grad = lax.dot_general(
            xv[t // 4, :, cols], grads[...], outer, preferred_element_type=F32
        ) * scale_in
        moment = momentum_beta * mgu[rows].astype(F32) + grad
        mgu[rows] = moment.astype(BF)
        lgu[rows] = (wgu[rows].astype(F32) - learn_rate * moment).astype(BF)
        for s in in_tile(t):
            s.start()
        return carry

    lax.fori_loop(0, 8, in_grads, 0)
    for load in loads[11:]:
        load.wait()

    def down_grads(c, carry):
        cols = pl.ds((c % 2) * 512, 512)
        where = pl.ds(c * 512, 512)
        grad = lax.dot_general(
            acv[...], yv[c // 2, :, cols], outer, preferred_element_type=F32
        ) * scale_hidden
        moment = momentum_beta * mdn[:, where].astype(F32) + grad
        mdn[:, where] = moment.astype(BF)
        ldn[:, where] = (wdn[:, where].astype(F32) - learn_rate * moment).astype(BF)
        for s in down_tile(c):
            s.start()
        return carry

    lax.fori_loop(0, 4, down_grads, 0)

    def back_rows(t, carry):
        part = pl.ds(t * 320, 320)
        inner = (((1,), (1,)), ((), ()))
        for r in range(2):
            back = lax.dot_general(
                grads[part], wgu[pl.ds(r * half, half)], inner, preferred_element_type=F32
            )
            xv[r, part] = (back * scale_in).astype(BF)
        return carry

    lax.fori_loop(0, 4, back_rows, 0)
    send_rows(1)
    moments = [
        pltpu.make_async_copy(s, d, go.at[i])
        for i, (s, d) in enumerate(((mgu, mgu_o), (mdn, md_o), (lgu, lgu_o), (ldn, ld_o)))
    ]
    for m in moments:
        m.start()

    def reduce(a):
        def body(i, carry):
            q = turn((i + 1) % 4)
            for r in range(2):
                group = (own[r] + q) % 4
                keep_copy(a, r, q).wait()
                for d in ORDER:
                    send_copy(a, r, q, d).wait_recv()
                hit, share = selection(mr, r, group)
                pick = (share if a == 0 else hit).astype(BF)
                for c in range(2):
                    part = pl.ds(c * (half // 2), half // 2)
                    rows = jnp.concatenate([rb[a, r, group, e, :, part] for e in range(4)], axis=0)
                    total = lax.dot_general(pick, rows, outer, preferred_element_type=F32)

                    @pl.when(i < 3)
                    def _():
                        qs[a, r, (q + 3) % 4, :, part] = total.astype(BF)

                    @pl.when(i == 3)
                    def _():
                        mine[r, :, part] = total

                @pl.when(i < 3)
                def _():
                    part_copy(a, r, q).start()
            return carry

        lax.fori_loop(0, 4, body, 0)
        there = pl.ds((1 - xh) * 128, 128)
        here = pl.ds(xh * 128, 128)
        for r in range(2):
            for q in ORDER:
                part_copy(a, r, q).wait_recv()
            away = mine[r, there]
            stay = mine[r, here]
            for q in ORDER:
                away = away + qr[a, r, q - 1, there].astype(F32)
                stay = stay + qr[a, r, q - 1, here].astype(F32)
            xsend[a, r] = away.astype(BF)
            x_copy(a, r).start()
            kept[a, r] = stay

    reduce(0)
    reduce(1)
    for a in range(2):
        for r in range(2):
            x_copy(a, r).wait_recv()
            total = kept[a, r] + xrecv[a, r].astype(F32)
            results[a][:, pl.ds(r * half, half)] = total.astype(BF)
    for a in range(2):
        for r in range(2):
            x_copy(a, r).wait_send()
            for q in range(4):
                for d in ORDER:
                    send_copy(a, r, q, d).wait_send()
            for q in ORDER:
                part_copy(a, r, q).wait_send()
    for t in range(8):
        for s in in_tile(t):
            s.wait()
    for c in range(4):
        for s in down_tile(c):
            s.wait()
    for m in moments:
        m.wait()


def combine(xi, yi, pr, aci, gri, mr, wg, wu, wd, mg, mu, md):
    half = xi.shape[2]
    width = 2 * half
    slots = xi.shape[1]
    hidden = wd.shape[0]
    dma = pltpu.SemaphoreType.DMA
    anywhere = pl.BlockSpec(memory_space=pl.ANY)
    vmem = pl.BlockSpec(memory_space=pltpu.VMEM)
    tokens = jax.ShapeDtypeStruct((128, width), BF)
    inward = jax.ShapeDtypeStruct((width, 2 * hidden), BF)
    down = jax.ShapeDtypeStruct((hidden, width), BF)
    return pl.pallas_call(
        combine_kernel,
        out_shape=(
            tokens, tokens, inward, down, inward, down,
            jax.ShapeDtypeStruct((2, width, 2 * hidden), BF),
            jax.ShapeDtypeStruct((2, hidden, width), BF),
        ),
        in_specs=[*[anywhere] * 5, vmem, *[anywhere] * 6],
        out_specs=(vmem, vmem, *[anywhere] * 6),
        scratch_shapes=[
            pltpu.VMEM((2, slots, half), BF),
            pltpu.VMEM((2, slots, half), BF),
            pltpu.VMEM((slots, hidden), BF),
            pltpu.VMEM((slots, 2 * hidden), BF),
            pltpu.VMEM((width, 2 * hidden), BF),
            pltpu.VMEM((hidden, width), BF),
            pltpu.VMEM((width, 2 * hidden), BF),
            pltpu.VMEM((hidden, width), BF),
            pltpu.VMEM((width, 2 * hidden), BF),
            pltpu.VMEM((hidden, width), BF),
            pltpu.VMEM((2, 2, 4, 4, 80, half), BF),
            pltpu.VMEM((2, 2, 3, 256, half), BF),
            pltpu.VMEM((2, 2, 3, 256, half), BF),
            pltpu.VMEM((2, 2, 128, half), BF),
            pltpu.VMEM((2, 2, 128, half), BF),
            pltpu.VMEM((2, 256, half), F32),
            pltpu.VMEM((2, 2, 128, half), F32),
            dma((2, 2, 4, 4)), dma((2, 2, 4, 4)),
            dma((2, 2, 4)),
            dma((2, 2, 4)), dma((2, 2, 4)),
            dma((2, 2)), dma((2, 2)),
            dma((2, 12)), dma((2, 12)),
            dma((15,)), dma((4,)),
        ],
        compiler_params=pltpu.CompilerParams(
            collective_id=1, has_side_effects=True, vmem_limit_bytes=63 * 2**20
        ),
        name="combine",
    )(xi, yi, pr, aci, gri, mr, wg, wu, wd, mg, mu, md)


def finish_kernel(
    bit, lgu, bgu, mgu, ld, bd, md, out, tg,
    ng, nu, nd, mgo, muo, mdo, oo, to,
):
    hidden = ng.shape[1]
    inward = ((lgu[...].astype(F32) + bgu[0].astype(F32)) * 0.5).astype(BF)
    ng[...] = inward[:, :hidden]
    nu[...] = inward[:, hidden:]
    nd[...] = ((ld[...].astype(F32) + bd[0].astype(F32)) * 0.5).astype(BF)
    mgo[...] = mgu[:, :hidden]
    muo[...] = mgu[:, hidden:]
    mdo[...] = md[...]
    oo[...] = out[...]
    to[...] = tg[...]


def finish(bit, lgu, bgu, mgu, ld, bd, md, out, tg):
    width, both = lgu.shape
    hidden = both // 2
    steps = 4
    tile = width // steps
    rows = pl.BlockSpec((tile, both), lambda i, b: (i, 0))
    half_rows = pl.BlockSpec((tile, hidden), lambda i, b: (i, 0))
    cols = pl.BlockSpec((hidden, tile), lambda i, b: (0, i))
    toks = pl.BlockSpec((128, tile), lambda i, b: (0, i))
    shape = jax.ShapeDtypeStruct
    return pl.pallas_call(
        finish_kernel,
        out_shape=(
            shape((width, hidden), BF), shape((width, hidden), BF), shape((hidden, width), BF),
            shape((width, hidden), BF), shape((width, hidden), BF), shape((hidden, width), BF),
            shape((128, width), BF), shape((128, width), BF),
        ),
        grid_spec=pltpu.PrefetchScalarGridSpec(
            num_scalar_prefetch=1,
            grid=(steps,),
            in_specs=[
                rows, pl.BlockSpec((1, tile, both), lambda i, b: (b[0], i, 0)), rows,
                cols, pl.BlockSpec((1, hidden, tile), lambda i, b: (b[0], 0, i)), cols,
                toks, toks,
            ],
            out_specs=(half_rows, half_rows, cols, half_rows, half_rows, cols, toks, toks),
        ),
        compiler_params=pltpu.CompilerParams(vmem_limit_bytes=62 * 2**20),
        name="finish",
    )(bit, lgu, bgu, mgu, ld, bd, md, out, tg)


def per_device(
    tokens, routing, gate_scores, cotangent,
    w_gate, w_up, w_down, mom_gate, mom_up, mom_down, gossip_round,
):
    wg, wu, wd = w_gate[0, 0], w_up[0, 0], w_down[0, 0]
    xi, yi, pr, aci, gri, meta = dispatch(
        tokens, cotangent, routing.T, gate_scores.T, wg, wu, wd
    )
    out, tg, lgu, ld, mgu, md, bgu, bd = combine(
        xi, yi, pr, aci, gri, meta, wg, wu, wd, mom_gate[0, 0], mom_up[0, 0], mom_down[0, 0]
    )
    ng, nu, nd, mg, mu, mdn, layer_out, token_grad = finish(
        gossip_round % 2, lgu, bgu, mgu, ld, bd, md, out, tg
    )
    return (
        layer_out, token_grad, ng[None, None], nu[None, None], nd[None, None],
        mg[None, None], mu[None, None], mdn[None, None],
    )


def solution(mesh):
    flat = P(("replica", "expert"), None)
    stacked = P("replica", "expert", None, None)
    return jax.shard_map(
        per_device,
        mesh=mesh,
        in_specs=(flat,) * 4 + (stacked,) * 6 + (P("expert"),),
        out_specs=(flat,) * 2 + (stacked,) * 6,
        check_vma=False,
    )
```

```python
import jax
import jax.numpy as jnp
from jax import lax
from jax.experimental import pallas as pl
from jax.experimental.pallas import tpu as pltpu
from jax.sharding import PartitionSpec as P

momentum_beta = 0.9
learn_rate = 0.1
MESH = pl.DeviceIdType.MESH
CAP = 40
BF = jnp.bfloat16
F32 = jnp.float32
ORDER = (1, 3, 2)
NEAR = (1, 3)


def place():
    e = lax.axis_index("expert")
    return e // 16, (e // 4) % 4, e % 4


def number(xh, z, y):
    return xh * 16 + z * 4 + y


def peer(route, stage, xh, z, y, d):
    if (route == 0) == (stage == 0):
        return number(xh, z, (y + d) % 4)
    return number(xh, (z + d) % 4, y)


def greet(ids):
    barrier = pltpu.get_barrier_semaphore()
    for where in ids:
        pl.semaphore_signal(barrier, inc=1, device_id=where, device_id_type=MESH)
    pl.semaphore_wait(barrier, len(ids))


def remote(src, dst, ss, rs, where):
    return pltpu.make_async_remote_copy(
        src_ref=src, dst_ref=dst, send_sem=ss, recv_sem=rs, device_id=where, device_id_type=MESH
    )


def turn(i):
    return i + i // 2 - 2 * (i // 3)


def selection(meta, route, group):
    width = 128
    rows = lax.broadcasted_iota(jnp.int32, (2 * CAP, width), 0).astype(F32)
    first = meta[route, group, 0]
    second = meta[route, group, 1]
    hits, shares = [], []
    for e in range(4):
        hit = jnp.concatenate(
            [rows == first[e : e + 1, :], rows == second[e : e + 1, :] + float(CAP)], axis=1
        )
        share = jnp.concatenate([first[4 + e : 5 + e, :], second[4 + e : 5 + e, :]], axis=1)
        hits.append(hit)
        shares.append(jnp.where(hit, share, 0.0))
    hit = jnp.concatenate([jnp.where(h, 1.0, 0.0) for h in hits], axis=0)
    return hit, jnp.concatenate(shares, axis=0)


def metadata(rt, gt, m1, m2):
    share = gt[...] / jnp.sum(gt[...], axis=0, keepdims=True)
    names = lax.broadcasted_iota(jnp.int32, (32, 128), 0)
    member = jnp.zeros((32, 128), F32)
    shares = jnp.zeros((32, 128), F32)
    for k in range(8):
        same = rt[k : k + 1, :] == names
        member = member + jnp.where(same, 1.0, 0.0)
        shares = shares + jnp.where(same, share[k : k + 1, :], 0.0)
    earlier_token = lax.broadcasted_iota(jnp.int32, (128, 128), 0)
    later_token = lax.broadcasted_iota(jnp.int32, (128, 128), 1)
    before = jnp.where(earlier_token < later_token, 1.0, 0.0).astype(BF)
    earlier = jnp.dot(member.astype(BF), before, preferred_element_type=F32)
    slots = jnp.where(member > 0.0, earlier, -1000.0)
    for xh in range(2):
        for i in range(4):
            for k in range(4):
                e1 = xh * 16 + k * 4 + i
                e2 = xh * 16 + i * 4 + k
                m1[xh, i, k : k + 1, :] = slots[e1 : e1 + 1]
                m1[xh, i, 4 + k : 5 + k, :] = shares[e1 : e1 + 1]
                m2[xh, i, k : k + 1, :] = slots[e2 : e2 + 1]
                m2[xh, i, 4 + k : 5 + k, :] = shares[e2 : e2 + 1]


def dispatch_kernel(
    tok, cot, rt, gt, wg, wu, wd,
    xo, yo, po, aco, gro, mo,
    ag, sb, xb, mr, m1, m2, wgu, wdn, gus, acs, prs, gas, grs,
    ms, mrs, xs, xr, gs, gr, us, ur, ls, lo, os_, wl, fo, hs, hr, go, ks, kr,
):
    xh, z, y = place()
    half = ag.shape[-1]
    hidden = wd.shape[0]
    scale_in = (2 * half) ** (-0.5)
    scale_hidden = hidden ** (-0.5)
    loads = [
        pltpu.make_async_copy(wg, wgu.at[:, pl.ds(0, hidden)], wl.at[0]),
        pltpu.make_async_copy(wu, wgu.at[:, pl.ds(hidden, hidden)], wl.at[1]),
        pltpu.make_async_copy(wd, wdn, wl.at[2]),
    ]
    others = []
    for dx in range(2):
        for d in range(4):
            if dx or d:
                others.append({"expert": number((xh + dx) % 2, z, (y + d) % 4)})
            if d:
                others.append({"expert": number((xh + dx) % 2, (z + d) % 4, y)})
    greet(others)
    own = (y, z)
    source = (tok, cot)
    partner = {"expert": number(1 - xh, z, y)}

    def cols(a, r):
        return source[a].at[:, pl.ds(r * half, half)]

    def x_copy(a, r):
        spot = ag.at[a, r, own[r], pl.ds(xh * 128, 128)]
        return remote(cols(a, r), spot, xs.at[a, r], xr.at[a, r], partner)

    def cross_copy(a, r, q):
        spot = ag.at[a, r, (own[r] + q) % 4, pl.ds(xh * 128, 128)]
        return remote(spot, spot, ks.at[a, r, q], kr.at[a, r, q], partner)

    def cross_wait(a, r, q):
        spot = ag.at[a, r, (own[r] + q) % 4, pl.ds((1 - xh) * 128, 128)]
        remote(spot, spot, ks.at[a, r, q], kr.at[a, r, q], partner).wait_recv()

    def own_copy(a, r):
        return pltpu.make_async_copy(
            cols(a, r), ag.at[a, r, own[r], pl.ds(xh * 128, 128)], ls.at[a, r]
        )

    def gather_copy(a, r, h, d):
        where = xh if h == 0 else 1 - xh
        spot = ag.at[a, r, own[r], pl.ds(where * 128, 128)]
        src = cols(a, r) if h == 0 else spot
        return remote(
            src, spot, gs.at[a, r, h, d], gr.at[a, r, h, d],
            {"expert": peer(r, 0, xh, z, y, d)},
        )

    def gather_wait(a, r, h, q):
        where = xh if h == 0 else 1 - xh
        spot = ag.at[a, r, (own[r] + q) % 4, pl.ds(where * 128, 128)]
        back = (4 - q) % 4
        remote(spot, spot, gs.at[a, r, h, back], gr.at[a, r, h, back], partner).wait_recv()

    def relay_copy(a, r, side):
        came, to = ((own[r] + 3) % 4, 1) if side == 0 else ((own[r] + 1) % 4, 3)
        spot = ag.at[a, r, came, pl.ds(xh * 128 + side * 64, 64)]
        return remote(
            spot, spot, hs.at[a, r, side], hr.at[a, r, side],
            {"expert": peer(r, 0, xh, z, y, to)},
        )

    def relay_wait(a, r, side):
        spot = ag.at[a, r, (own[r] + 2) % 4, pl.ds(xh * 128 + side * 64, 64)]
        remote(spot, spot, hs.at[a, r, side], hr.at[a, r, side], partner).wait_recv()

    def relay(a):
        for r in range(2):
            gather_wait(a, r, 0, 3)
            relay_copy(a, r, 0).start()
            gather_wait(a, r, 0, 1)
            relay_copy(a, r, 1).start()

    def landing(a, r, sender, group):
        row = (sender * 4 + group) if r == 0 else (group * 4 + sender)
        return xb.at[a, r, pl.ds(row * 80, 80)]

    def spread_copy(a, r, q, d):
        group = (own[r] + q) % 4
        me = own[1 - r]
        return remote(
            sb.at[a, r, (me + d) % 4, q], landing(a, r, me, group),
            us.at[a, r, q, d], ur.at[a, r, q, d],
            {"expert": peer(r, 1, xh, z, y, d)},
        )

    def keep_copy(a, r, q):
        group = (own[r] + q) % 4
        me = own[1 - r]
        return pltpu.make_async_copy(sb.at[a, r, me, q], landing(a, r, me, group), lo.at[a, r, q])

    metas = (m1, m2)

    def meta_copy(r, dx, d):
        to_x = (xh + dx) % 2
        to = (own[r] + d) % 4
        where = number(to_x, z, to) if r == 0 else number(to_x, to, y)
        return remote(
            metas[r].at[to_x, to], mr.at[r, own[r], xh], ms.at[r, dx, d], mrs.at[r, dx, d],
            {"expert": where},
        )

    for r in range(2):
        x_copy(0, r).start()
        own_copy(0, r).start()
    for d in NEAR:
        for r in range(2):
            gather_copy(0, r, 0, d).start()
    for r in range(2):
        x_copy(1, r).start()
        own_copy(1, r).start()
    for d in NEAR:
        for r in range(2):
            gather_copy(1, r, 0, d).start()
    for load in loads:
        load.start()
    pairs = [(dx, d) for dx in range(2) for d in range(4) if dx or d]
    metadata(rt, gt, m1, m2)
    for r in range(2):
        mr[r, own[r], xh] = metas[r][xh, own[r]]
    for r in range(2):
        for dx, d in pairs:
            meta_copy(r, dx, d).start()

    def pass_on(a):
        for r in range(2):
            own_copy(a, r).wait()
            spot = ag.at[a, r, own[r], pl.ds((1 - xh) * 128, 128)]
            remote(spot, spot, xs.at[a, r], xr.at[a, r], partner).wait_recv()
            if a == 0:
                for d in NEAR:
                    gather_copy(a, r, 1, d).start()

    def cross_far(a):
        for r in range(2):
            for side in range(2):
                relay_wait(a, r, side)
            cross_copy(a, r, 2).start()

    relay(0)
    pass_on(0)
    cross_far(0)
    relay(1)
    for q in NEAR:
        for r in range(2):
            cross_copy(1, r, q).start()
    for r in range(2):
        for dx, d in pairs:
            meta_copy(r, dx, d).wait()

    def spread(a):
        def body(i, carry):
            q = turn(i)

            if a == 0:

                @pl.when(i == 1)
                def _():
                    for r in range(2):
                        for k in NEAR:
                            gather_wait(0, r, 1, k)

                @pl.when(i == 2)
                def _():
                    cross_far(1)

            for r in range(2):
                group = (own[r] + q) % 4

                if a == 0:

                    @pl.when(i == 3)
                    def _():
                        cross_wait(0, r, 2)

                else:

                    @pl.when(i > 0)
                    def _():
                        cross_wait(1, r, q)

                hit, share = selection(mr, r, group)
                hit = hit.astype(BF)
                for c in range(2):
                    part = pl.ds(c * (half // 2), half // 2)
                    rows = jnp.dot(hit, ag[a, r, group, :, part], preferred_element_type=F32)
                    if a == 1:
                        rows = rows * jnp.sum(share, axis=1, keepdims=True)
                    rows = rows.astype(BF)
                    for e in range(4):
                        sb[a, r, e, q, :, part] = rows[e * 80 : e * 80 + 80]
                for d in ORDER:
                    spread_copy(a, r, q, d).start()
                keep_copy(a, r, q).start()
            return carry

        lax.fori_loop(0, 4, body, 0)

    spread(0)
    pass_on(1)
    spread(1)
    results = (xo, yo)

    def landed(a, r, q):
        keep_copy(a, r, q).wait()
        for d in ORDER:
            spread_copy(a, r, q, d).wait()

    def leave(a, r):
        pltpu.make_async_copy(xb.at[a, r], results[a].at[r], os_.at[a, r]).start()

    for r in range(2):
        for q in range(4):
            landed(0, r, q)
        leave(0, r)
    for load in loads:
        load.wait()

    def stores(t):
        part = pl.ds(t * 320, 320)
        found = [
            pltpu.make_async_copy(acs.at[part], aco.at[part], fo.at[t, 0]),
        ]
        for r in range(2):
            found.append(pltpu.make_async_copy(prs.at[r, part], po.at[r, part], fo.at[t, 1 + r]))
        return found

    def forward(t, carry):
        part = pl.ds(t * 320, 320)
        both = jnp.dot(xb[0, 0, part], wgu[pl.ds(0, half)], preferred_element_type=F32)
        both = both + jnp.dot(xb[0, 1, part], wgu[pl.ds(half, half)], preferred_element_type=F32)
        both = both * scale_in
        gus[part] = both
        gate = both[:, :hidden]
        act = (gate * jax.nn.sigmoid(gate) * both[:, hidden:]).astype(BF)
        acs[part] = act
        for r in range(2):
            made = jnp.dot(act, wdn[:, pl.ds(r * half, half)], preferred_element_type=F32)
            prs[r, part] = (made * scale_hidden).astype(BF)
        for s in stores(t):
            s.start()
        return carry

    lax.fori_loop(0, 4, forward, 0)
    gas[...] = jnp.zeros_like(gas)
    inner = (((1,), (1,)), ((), ()))

    def grad_part(i, carry):
        q = turn(i)
        landed(1, 0, q)
        spots = [pl.ds((k * 4 + (y + q) % 4) * 80, 80) for k in range(4)]
        rows = jnp.concatenate([xb[1, 0, s] for s in spots], axis=0)
        more = lax.dot_general(rows, wdn[:, pl.ds(0, half)], inner, preferred_element_type=F32)
        for k, s in enumerate(spots):
            gas[s] += more[k * 80 : k * 80 + 80]
        landed(1, 1, q)
        part = pl.ds(((z + q) % 4) * 320, 320)
        gas[part] += lax.dot_general(
            xb[1, 1, part], wdn[:, pl.ds(half, half)], inner, preferred_element_type=F32
        )
        return carry

    lax.fori_loop(0, 4, grad_part, 0)
    for r in range(2):
        leave(1, r)
    mo[...] = mr[...]

    def grad_store(t):
        part = pl.ds(t * 160, 160)
        return pltpu.make_async_copy(grs.at[part], gro.at[part], go.at[t])

    def hidden_grads(t, carry):
        part = pl.ds(t * 160, 160)
        grad_act = gas[part] * scale_hidden
        gate = gus[part, pl.ds(0, hidden)]
        up = gus[part, pl.ds(hidden, hidden)]
        sig = jax.nn.sigmoid(gate)
        grs[part, pl.ds(0, hidden)] = (
            grad_act * up * sig * (1.0 + gate * (1.0 - sig))
        ).astype(BF)
        grs[part, pl.ds(hidden, hidden)] = (grad_act * gate * sig).astype(BF)
        grad_store(t).start()
        return carry

    lax.fori_loop(0, 8, hidden_grads, 0)
    for t in range(8):
        grad_store(t).wait()
    for r in range(2):
        cross_copy(0, r, 2).wait_send()
        for q in ORDER:
            cross_copy(1, r, q).wait_send()
    for t in range(4):
        for s in stores(t):
            s.wait()
    for a in range(2):
        for r in range(2):
            x_copy(a, r).wait_send()
            for h in range(2 - a):
                for d in NEAR:
                    gather_copy(a, r, h, d).wait_send()
            for side in range(2):
                relay_copy(a, r, side).wait_send()
            pltpu.make_async_copy(xb.at[a, r], results[a].at[r], os_.at[a, r]).wait()


def dispatch(tokens, cotangent, rt, gt, wg, wu, wd):
    rows, width = tokens.shape
    half = width // 2
    hidden = wd.shape[0]
    dma = pltpu.SemaphoreType.DMA
    anywhere = pl.BlockSpec(memory_space=pl.ANY)
    vmem = pl.BlockSpec(memory_space=pltpu.VMEM)
    slots = 32 * CAP
    halves = jax.ShapeDtypeStruct((2, slots, half), BF)
    return pl.pallas_call(
        dispatch_kernel,
        out_shape=(
            halves, halves, halves,
            jax.ShapeDtypeStruct((slots, hidden), BF),
            jax.ShapeDtypeStruct((slots, 2 * hidden), BF),
            jax.ShapeDtypeStruct((2, 4, 2, 8, 128), F32),
        ),
        in_specs=[anywhere, anywhere, vmem, vmem, anywhere, anywhere, anywhere],
        out_specs=(*[anywhere] * 5, vmem),
        scratch_shapes=[
            pltpu.VMEM((2, 2, 4, 256, half), BF),
            pltpu.VMEM((2, 2, 4, 4, 80, half), BF),
            pltpu.VMEM((2, 2, slots, half), BF),
            pltpu.VMEM((2, 4, 2, 8, 128), F32),
            pltpu.VMEM((2, 4, 8, 128), F32),
            pltpu.VMEM((2, 4, 8, 128), F32),
            pltpu.VMEM((width, 2 * hidden), BF),
            pltpu.VMEM((hidden, width), BF),
            pltpu.VMEM((slots, 2 * hidden), F32),
            pltpu.VMEM((slots, hidden), BF),
            pltpu.VMEM((2, slots, half), BF),
            pltpu.VMEM((slots, hidden), F32),
            pltpu.VMEM((slots, 2 * hidden), BF),
            dma((2, 2, 4)), dma((2, 2, 4)),
            dma((2, 2)), dma((2, 2)),
            dma((2, 2, 2, 4)), dma((2, 2, 2, 4)),
            dma((2, 2, 4, 4)), dma((2, 2, 4, 4)),
            dma((2, 2)), dma((2, 2, 4)), dma((2, 2)),
            dma((3,)), dma((4, 3)),
            dma((2, 2, 2)), dma((2, 2, 2)), dma((8,)),
            dma((2, 2, 4)), dma((2, 2, 4)),
        ],
        compiler_params=pltpu.CompilerParams(
            collective_id=0, has_side_effects=True, vmem_limit_bytes=60 * 2**20
        ),
        name="dispatch",
    )(tokens, cotangent, rt, gt, wg, wu, wd)


def combine_kernel(
    bit, xi, yi, pr, aci, gri, mr, wg, wu, wd, mg, mu, md,
    out, tg, ngu_o, nd_o, mgu_o, md_o, bgu, bd,
    xv, yv, acv, grads, wgu, wdn, mgu, mdn, lgu, ldn, fgu, fdn,
    rb, qs, qr, xsend, xrecv, mine, kept,
    cs, cr, ls, ps, pt, xs, xr, ws, wr, wl, go, nl, av,
):
    xh, z, y = place()
    rep = lax.axis_index("replica")
    half = rb.shape[-1]
    hidden = wd.shape[0]
    scale_in = (2 * half) ** (-0.5)
    scale_hidden = hidden ** (-0.5)
    low, high = pl.ds(0, hidden), pl.ds(hidden, hidden)
    copies = [(gri, grads)]
    for k in range(2):
        rows = pl.ds(k * half, half)
        copies.append((xi.at[k], xv.at[k]))
        for src, dst, cols in ((mg, mgu, low), (mu, mgu, high), (wg, wgu, low), (wu, wgu, high)):
            copies.append((src.at[rows], dst.at[rows, cols]))
    copies += [(aci, acv), (yi, yv), (md, mdn), (wd, wdn)]
    loads = [pltpu.make_async_copy(s, d, wl.at[i]) for i, (s, d) in enumerate(copies)]
    for load in loads:
        load.start()
    own = (y, z)
    partner = {"expert": number(1 - xh, z, y)}
    core_mate = {"replica": rep + 1 - 2 * (rep % 2)}
    far_mate = {"replica": (rep + 2) % 4}
    others = [partner, core_mate, far_mate]
    for d in ORDER:
        others.append({"expert": number(xh, z, (y + d) % 4)})
        others.append({"expert": number(xh, (z + d) % 4, y)})
    greet(others)
    source = (pr, xv)
    results = (out, tg)

    def block(a, r, e, group):
        row = (e * 4 + group) if r == 0 else (group * 4 + e)
        return source[a].at[r, pl.ds(row * 80, 80)]

    def send_copy(a, r, q, d):
        group = (own[r] + q) % 4
        me = own[1 - r]
        return remote(
            block(a, r, (me + d) % 4, group), rb.at[a, r, group, me],
            cs.at[a, r, q, d], cr.at[a, r, q, d],
            {"expert": peer(r, 1, xh, z, y, d)},
        )

    def keep_copy(a, r, q):
        group = (own[r] + q) % 4
        me = own[1 - r]
        return pltpu.make_async_copy(block(a, r, me, group), rb.at[a, r, group, me], ls.at[a, r, q])

    def part_copy(a, r, q):
        return remote(
            qs.at[a, r, q - 1], qr.at[a, r, q - 1], ps.at[a, r, q], pt.at[a, r, q],
            {"expert": peer(r, 0, xh, z, y, q)},
        )

    def x_copy(a, r):
        return remote(xsend.at[a, r], xrecv.at[a, r], xs.at[a, r], xr.at[a, r], partner)

    def send_rows(a):
        for q in (1, 3, 2, 0):
            for r in range(2):
                keep_copy(a, r, q).start()
            for d in ORDER:
                for r in range(2):
                    send_copy(a, r, q, d).start()

    def in_tile(t):
        rows = pl.ds(t * 256, 256)
        src = lgu.at[rows]
        return [
            remote(src, fgu.at[rows], ws.at[1, t], wr.at[1, t], far_mate),
            remote(src, bgu.at[rows], ws.at[0, t], wr.at[0, t], core_mate),
        ]

    def down_tile(c):
        cols = pl.ds(c * 512, 512)
        src = ldn.at[:, cols]
        return [
            remote(src, fdn.at[:, cols], ws.at[1, 8 + c], wr.at[1, 8 + c], far_mate),
            remote(src, bd.at[:, cols], ws.at[0, 8 + c], wr.at[0, 8 + c], core_mate),
        ]

    send_rows(0)
    for load in loads[:6]:
        load.wait()
    outer = (((0,), (0,)), ((), ()))

    def in_grads(t, carry):
        @pl.when(t == 4)
        def _():
            for load in loads[6:11]:
                load.wait()

        rows = pl.ds(t * 256, 256)
        cols = pl.ds((t % 4) * 256, 256)
        grad = lax.dot_general(
            xv[t // 4, :, cols], grads[...], outer, preferred_element_type=F32
        ) * scale_in
        moment = momentum_beta * mgu[rows].astype(F32) + grad
        mgu[rows] = moment.astype(BF)
        lgu[rows] = (wgu[rows].astype(F32) - learn_rate * moment).astype(BF)
        for s in in_tile(t):
            s.start()
        return carry

    lax.fori_loop(0, 8, in_grads, 0)
    for load in loads[11:]:
        load.wait()

    def down_grads(c, carry):
        cols = pl.ds((c % 2) * 512, 512)
        where = pl.ds(c * 512, 512)
        grad = lax.dot_general(
            acv[...], yv[c // 2, :, cols], outer, preferred_element_type=F32
        ) * scale_hidden
        moment = momentum_beta * mdn[:, where].astype(F32) + grad
        mdn[:, where] = moment.astype(BF)
        ldn[:, where] = (wdn[:, where].astype(F32) - learn_rate * moment).astype(BF)
        for s in down_tile(c):
            s.start()
        return carry

    lax.fori_loop(0, 4, down_grads, 0)

    def back_rows(t, carry):
        part = pl.ds(t * 320, 320)
        inner = (((1,), (1,)), ((), ()))
        for r in range(2):
            back = lax.dot_general(
                grads[part], wgu[pl.ds(r * half, half)], inner, preferred_element_type=F32
            )
            xv[r, part] = (back * scale_in).astype(BF)
        return carry

    lax.fori_loop(0, 4, back_rows, 0)
    send_rows(1)
    moments = [
        pltpu.make_async_copy(s, d, go.at[i])
        for i, (s, d) in enumerate(((mgu, mgu_o), (mdn, md_o)))
    ]
    for m in moments:
        m.start()

    def reduce(a):
        def body(i, carry):
            q = turn((i + 1) % 4)
            for r in range(2):
                group = (own[r] + q) % 4
                keep_copy(a, r, q).wait()
                for d in ORDER:
                    send_copy(a, r, q, d).wait_recv()
                hit, share = selection(mr, r, group)
                pick = (share if a == 0 else hit).astype(BF)
                for c in range(2):
                    part = pl.ds(c * (half // 2), half // 2)
                    rows = jnp.concatenate([rb[a, r, group, e, :, part] for e in range(4)], axis=0)
                    total = lax.dot_general(pick, rows, outer, preferred_element_type=F32)

                    @pl.when(i < 3)
                    def _():
                        qs[a, r, (q + 3) % 4, :, part] = total.astype(BF)

                    @pl.when(i == 3)
                    def _():
                        mine[r, :, part] = total

                @pl.when(i < 3)
                def _():
                    part_copy(a, r, q).start()
            return carry

        lax.fori_loop(0, 4, body, 0)
        there = pl.ds((1 - xh) * 128, 128)
        here = pl.ds(xh * 128, 128)
        for r in range(2):
            for q in ORDER:
                part_copy(a, r, q).wait_recv()
            away = mine[r, there]
            stay = mine[r, here]
            for q in ORDER:
                away = away + qr[a, r, q - 1, there].astype(F32)
                stay = stay + qr[a, r, q - 1, here].astype(F32)
            xsend[a, r] = away.astype(BF)
            x_copy(a, r).start()
            kept[a, r] = stay

    reduce(0)
    for t in range(8):
        in_tile(t)[1].wait_recv()
    for c in range(4):
        down_tile(c)[1].wait_recv()
    near = [
        pltpu.make_async_copy(bgu, wgu, nl.at[0]),
        pltpu.make_async_copy(bd, wdn, nl.at[1]),
    ]
    for n in near:
        n.start()
    reduce(1)
    for n in near:
        n.wait()
    pick = bit[0] % 2 == 0

    def in_store(t):
        rows = pl.ds(t * 256, 256)
        return pltpu.make_async_copy(lgu.at[rows], ngu_o.at[rows], av.at[t])

    def down_store(c):
        cols = pl.ds(c * 512, 512)
        return pltpu.make_async_copy(ldn.at[:, cols], nd_o.at[:, cols], av.at[8 + c])

    def in_average(t, carry):
        far, close = in_tile(t)
        far.wait()
        close.wait_send()
        rows = pl.ds(t * 256, 256)
        other = jnp.where(pick, wgu[rows].astype(F32), fgu[rows].astype(F32))
        lgu[rows] = ((lgu[rows].astype(F32) + other) * 0.5).astype(BF)
        in_store(t).start()
        return carry

    def down_average(c, carry):
        far, close = down_tile(c)
        far.wait()
        close.wait_send()
        cols = pl.ds(c * 512, 512)
        other = jnp.where(pick, wdn[:, cols].astype(F32), fdn[:, cols].astype(F32))
        ldn[:, cols] = ((ldn[:, cols].astype(F32) + other) * 0.5).astype(BF)
        down_store(c).start()
        return carry

    lax.fori_loop(0, 8, in_average, 0)
    lax.fori_loop(0, 4, down_average, 0)
    for a in range(2):
        for r in range(2):
            x_copy(a, r).wait_recv()
            total = kept[a, r] + xrecv[a, r].astype(F32)
            results[a][:, pl.ds(r * half, half)] = total.astype(BF)
    for a in range(2):
        for r in range(2):
            x_copy(a, r).wait_send()
            for q in range(4):
                for d in ORDER:
                    send_copy(a, r, q, d).wait_send()
            for q in ORDER:
                part_copy(a, r, q).wait_send()
    for t in range(8):
        in_store(t).wait()
    for c in range(4):
        down_store(c).wait()
    for m in moments:
        m.wait()


def combine(bit, xi, yi, pr, aci, gri, mr, wg, wu, wd, mg, mu, md):
    half = xi.shape[2]
    width = 2 * half
    slots = xi.shape[1]
    hidden = wd.shape[0]
    dma = pltpu.SemaphoreType.DMA
    anywhere = pl.BlockSpec(memory_space=pl.ANY)
    vmem = pl.BlockSpec(memory_space=pltpu.VMEM)
    tokens = jax.ShapeDtypeStruct((128, width), BF)
    inward = jax.ShapeDtypeStruct((width, 2 * hidden), BF)
    down = jax.ShapeDtypeStruct((hidden, width), BF)
    return pl.pallas_call(
        combine_kernel,
        out_shape=(
            tokens, tokens, inward, down, inward, down, inward, down,
        ),
        in_specs=[pl.BlockSpec(memory_space=pltpu.SMEM), *[anywhere] * 5, vmem, *[anywhere] * 6],
        out_specs=(vmem, vmem, *[anywhere] * 6),
        scratch_shapes=[
            pltpu.VMEM((2, slots, half), BF),
            pltpu.VMEM((2, slots, half), BF),
            pltpu.VMEM((slots, hidden), BF),
            pltpu.VMEM((slots, 2 * hidden), BF),
            pltpu.VMEM((width, 2 * hidden), BF),
            pltpu.VMEM((hidden, width), BF),
            pltpu.VMEM((width, 2 * hidden), BF),
            pltpu.VMEM((hidden, width), BF),
            pltpu.VMEM((width, 2 * hidden), BF),
            pltpu.VMEM((hidden, width), BF),
            pltpu.VMEM((width, 2 * hidden), BF),
            pltpu.VMEM((hidden, width), BF),
            pltpu.VMEM((2, 2, 4, 4, 80, half), BF),
            pltpu.VMEM((2, 2, 3, 256, half), BF),
            pltpu.VMEM((2, 2, 3, 256, half), BF),
            pltpu.VMEM((2, 2, 128, half), BF),
            pltpu.VMEM((2, 2, 128, half), BF),
            pltpu.VMEM((2, 256, half), F32),
            pltpu.VMEM((2, 2, 128, half), F32),
            dma((2, 2, 4, 4)), dma((2, 2, 4, 4)),
            dma((2, 2, 4)),
            dma((2, 2, 4)), dma((2, 2, 4)),
            dma((2, 2)), dma((2, 2)),
            dma((2, 12)), dma((2, 12)),
            dma((15,)), dma((2,)), dma((2,)), dma((12,)),
        ],
        compiler_params=pltpu.CompilerParams(
            collective_id=1, has_side_effects=True, vmem_limit_bytes=63 * 2**20
        ),
        name="combine",
    )(bit, xi, yi, pr, aci, gri, mr, wg, wu, wd, mg, mu, md)


def finish_kernel(
    ngu, mgu, nd, md, out, tg, ngo, nuo, ndo, mgo, muo, mdo, oo, to,
    v0, v1, v2, v3, v4, v5, gets, puts,
):
    hidden = ngo.shape[1]
    whole = pl.ds(0, nd.shape[1])
    left, right = pl.ds(0, hidden), pl.ds(hidden, hidden)
    parts = 4
    pieces = []
    for k in range(parts):
        for src, buf, ends in (
            (ngu, v0, ((left, ngo), (right, nuo))), (mgu, v1, ((left, mgo), (right, muo))),
            (nd, v2, ((whole, ndo),)), (md, v3, ((whole, mdo),)),
            (out, v4, ((whole, oo),)), (tg, v5, ((whole, to),)),
        ):
            size = src.shape[0] // parts
            pieces.append((src, buf, pl.ds(k * size, size), ends))
    loads, stores = [], []
    for n, (src, buf, rows, ends) in enumerate(pieces):
        loads.append(pltpu.make_async_copy(src.at[rows], buf.at[rows], gets.at[n]))
        stores.append([
            pltpu.make_async_copy(buf.at[rows, cols], dst.at[rows], puts.at[n, i])
            for i, (cols, dst) in enumerate(ends)
        ])
    for load in loads:
        load.start()
    for load, ends in zip(loads, stores):
        load.wait()
        for store in ends:
            store.start()
    for ends in stores:
        for store in ends:
            store.wait()


def finish(ngu, mgu, nd, md, out, tg):
    width, both = ngu.shape
    hidden = both // 2
    shape = jax.ShapeDtypeStruct
    anywhere = pl.BlockSpec(memory_space=pl.ANY)
    inputs = (ngu, mgu, nd, md, out, tg)
    return pl.pallas_call(
        finish_kernel,
        out_shape=(
            shape((width, hidden), BF), shape((width, hidden), BF), shape((hidden, width), BF),
            shape((width, hidden), BF), shape((width, hidden), BF), shape((hidden, width), BF),
            shape((128, width), BF), shape((128, width), BF),
        ),
        in_specs=[anywhere] * 6,
        out_specs=(anywhere,) * 8,
        scratch_shapes=[
            *[pltpu.VMEM(v.shape, BF) for v in inputs],
            pltpu.SemaphoreType.DMA((24,)), pltpu.SemaphoreType.DMA((24, 2)),
        ],
        compiler_params=pltpu.CompilerParams(vmem_limit_bytes=62 * 2**20),
        name="finish",
    )(*inputs)


def per_device(
    tokens, routing, gate_scores, cotangent,
    w_gate, w_up, w_down, mom_gate, mom_up, mom_down, gossip_round,
):
    wg, wu, wd = w_gate[0, 0], w_up[0, 0], w_down[0, 0]
    xi, yi, pr, aci, gri, meta = dispatch(
        tokens, cotangent, routing.T, gate_scores.T, wg, wu, wd
    )
    out, tg, ngu, nd, mgu, md, _, _ = combine(
        gossip_round, xi, yi, pr, aci, gri, meta, wg, wu, wd,
        mom_gate[0, 0], mom_up[0, 0], mom_down[0, 0],
    )
    ng, nu, nd, mg, mu, mdn, layer_out, token_grad = finish(ngu, mgu, nd, md, out, tg)
    return (
        layer_out, token_grad, ng[None, None], nu[None, None], nd[None, None],
        mg[None, None], mu[None, None], mdn[None, None],
    )


def solution(mesh):
    flat = P(("replica", "expert"), None)
    stacked = P("replica", "expert", None, None)
    return jax.shard_map(
        per_device,
        mesh=mesh,
        in_specs=(flat,) * 4 + (stacked,) * 6 + (P("expert"),),
        out_specs=(flat,) * 2 + (stacked,) * 6,
        check_vma=False,
    )
```

```python
import jax
import jax.numpy as jnp
from jax import lax
from jax.experimental import pallas as pl
from jax.experimental.pallas import tpu as pltpu
from jax.sharding import PartitionSpec as P

momentum_beta = 0.9
learn_rate = 0.1
MESH = pl.DeviceIdType.MESH
CAP = 40
BF = jnp.bfloat16
F32 = jnp.float32
ORDER = (1, 3, 2)
NEAR = (1, 3)


def place():
    e = lax.axis_index("expert")
    return e // 16, (e // 4) % 4, e % 4


def number(xh, z, y):
    return xh * 16 + z * 4 + y


def peer(route, stage, xh, z, y, d):
    if (route == 0) == (stage == 0):
        return number(xh, z, (y + d) % 4)
    return number(xh, (z + d) % 4, y)


def greet(ids):
    barrier = pltpu.get_barrier_semaphore()
    for where in ids:
        pl.semaphore_signal(barrier, inc=1, device_id=where, device_id_type=MESH)
    pl.semaphore_wait(barrier, len(ids))


def remote(src, dst, ss, rs, where):
    return pltpu.make_async_remote_copy(
        src_ref=src, dst_ref=dst, send_sem=ss, recv_sem=rs, device_id=where, device_id_type=MESH
    )


def turn(i):
    return i + i // 2 - 2 * (i // 3)


def selection(meta, route, group):
    width = 128
    rows = lax.broadcasted_iota(jnp.int32, (2 * CAP, width), 0).astype(F32)
    first = meta[route, group, 0]
    second = meta[route, group, 1]
    hits, shares = [], []
    for e in range(4):
        hit = jnp.concatenate(
            [rows == first[e : e + 1, :], rows == second[e : e + 1, :] + float(CAP)], axis=1
        )
        share = jnp.concatenate([first[4 + e : 5 + e, :], second[4 + e : 5 + e, :]], axis=1)
        hits.append(hit)
        shares.append(jnp.where(hit, share, 0.0))
    hit = jnp.concatenate([jnp.where(h, 1.0, 0.0) for h in hits], axis=0)
    return hit, jnp.concatenate(shares, axis=0)


def metadata(rt, gt, m1, m2):
    share = gt[...] / jnp.sum(gt[...], axis=0, keepdims=True)
    names = lax.broadcasted_iota(jnp.int32, (32, 128), 0)
    member = jnp.zeros((32, 128), F32)
    shares = jnp.zeros((32, 128), F32)
    for k in range(8):
        same = rt[k : k + 1, :] == names
        member = member + jnp.where(same, 1.0, 0.0)
        shares = shares + jnp.where(same, share[k : k + 1, :], 0.0)
    earlier_token = lax.broadcasted_iota(jnp.int32, (128, 128), 0)
    later_token = lax.broadcasted_iota(jnp.int32, (128, 128), 1)
    before = jnp.where(earlier_token < later_token, 1.0, 0.0).astype(BF)
    earlier = jnp.dot(member.astype(BF), before, preferred_element_type=F32)
    slots = jnp.where(member > 0.0, earlier, -1000.0)
    for xh in range(2):
        for i in range(4):
            for k in range(4):
                e1 = xh * 16 + k * 4 + i
                e2 = xh * 16 + i * 4 + k
                m1[xh, i, k : k + 1, :] = slots[e1 : e1 + 1]
                m1[xh, i, 4 + k : 5 + k, :] = shares[e1 : e1 + 1]
                m2[xh, i, k : k + 1, :] = slots[e2 : e2 + 1]
                m2[xh, i, 4 + k : 5 + k, :] = shares[e2 : e2 + 1]


def dispatch_kernel(
    tok, cot, rt, gt, wg, wu, wd,
    xo, yo, po, aco, gro, mo,
    ag, sb, xb, mr, m1, m2, wgu, wdn, gus, acs, prs, gas, grs,
    ms, mrs, xs, xr, gs, gr, us, ur, ls, lo, os_, wl, fo, hs, hr, go, ks, kr, lv,
):
    xh, z, y = place()
    half = ag.shape[-1]
    hidden = wd.shape[0]
    scale_in = (2 * half) ** (-0.5)
    scale_hidden = hidden ** (-0.5)
    loads = [
        pltpu.make_async_copy(wg, wgu.at[:, pl.ds(0, hidden)], wl.at[0]),
        pltpu.make_async_copy(wu, wgu.at[:, pl.ds(hidden, hidden)], wl.at[1]),
        pltpu.make_async_copy(wd, wdn, wl.at[2]),
    ]
    others = []
    for dx in range(2):
        for d in range(4):
            if dx or d:
                others.append({"expert": number((xh + dx) % 2, z, (y + d) % 4)})
            if d:
                others.append({"expert": number((xh + dx) % 2, (z + d) % 4, y)})
    greet(others)
    own = (y, z)
    source = (tok, cot)
    partner = {"expert": number(1 - xh, z, y)}

    def cols(a, r):
        return source[a].at[:, pl.ds(r * half, half)]

    def x_copy(a, r):
        spot = ag.at[a, r, own[r], pl.ds(xh * 128, 128)]
        return remote(cols(a, r), spot, xs.at[a, r], xr.at[a, r], partner)

    def cross_copy(a, r, q):
        spot = ag.at[a, r, (own[r] + q) % 4, pl.ds(xh * 128, 128)]
        return remote(spot, spot, ks.at[a, r, q], kr.at[a, r, q], partner)

    def cross_wait(a, r, q):
        spot = ag.at[a, r, (own[r] + q) % 4, pl.ds((1 - xh) * 128, 128)]
        remote(spot, spot, ks.at[a, r, q], kr.at[a, r, q], partner).wait_recv()

    def own_copy(a, r):
        return pltpu.make_async_copy(
            cols(a, r), ag.at[a, r, own[r], pl.ds(xh * 128, 128)], ls.at[a, r]
        )

    def gather_copy(a, r, h, d):
        where = xh if h == 0 else 1 - xh
        spot = ag.at[a, r, own[r], pl.ds(where * 128, 128)]
        src = cols(a, r) if h == 0 else spot
        return remote(
            src, spot, gs.at[a, r, h, d], gr.at[a, r, h, d],
            {"expert": peer(r, 0, xh, z, y, d)},
        )

    def gather_wait(a, r, h, q):
        where = xh if h == 0 else 1 - xh
        spot = ag.at[a, r, (own[r] + q) % 4, pl.ds(where * 128, 128)]
        back = (4 - q) % 4
        remote(spot, spot, gs.at[a, r, h, back], gr.at[a, r, h, back], partner).wait_recv()

    def relay_copy(a, r, side):
        came, to = ((own[r] + 3) % 4, 1) if side == 0 else ((own[r] + 1) % 4, 3)
        spot = ag.at[a, r, came, pl.ds(xh * 128 + side * 64, 64)]
        return remote(
            spot, spot, hs.at[a, r, side], hr.at[a, r, side],
            {"expert": peer(r, 0, xh, z, y, to)},
        )

    def relay_wait(a, r, side):
        spot = ag.at[a, r, (own[r] + 2) % 4, pl.ds(xh * 128 + side * 64, 64)]
        remote(spot, spot, hs.at[a, r, side], hr.at[a, r, side], partner).wait_recv()

    def relay(a):
        for r in range(2):
            gather_wait(a, r, 0, 3)
            relay_copy(a, r, 0).start()
            gather_wait(a, r, 0, 1)
            relay_copy(a, r, 1).start()

    def landing(a, r, sender, group):
        row = (sender * 4 + group) if r == 0 else (group * 4 + sender)
        return xb.at[a, r, pl.ds(row * 80, 80)]

    def spread_copy(a, r, q, d):
        group = (own[r] + q) % 4
        me = own[1 - r]
        return remote(
            sb.at[a, r, (me + d) % 4, q], landing(a, r, me, group),
            us.at[a, r, q, d], ur.at[a, r, q, d],
            {"expert": peer(r, 1, xh, z, y, d)},
        )

    def keep_copy(a, r, q):
        group = (own[r] + q) % 4
        me = own[1 - r]
        return pltpu.make_async_copy(sb.at[a, r, me, q], landing(a, r, me, group), lo.at[a, r, q])

    metas = (m1, m2)

    def meta_copy(r, dx, d):
        to_x = (xh + dx) % 2
        to = (own[r] + d) % 4
        where = number(to_x, z, to) if r == 0 else number(to_x, to, y)
        return remote(
            metas[r].at[to_x, to], mr.at[r, own[r], xh], ms.at[r, dx, d], mrs.at[r, dx, d],
            {"expert": where},
        )

    for r in range(2):
        x_copy(0, r).start()
        own_copy(0, r).start()
    for d in NEAR:
        for r in range(2):
            gather_copy(0, r, 0, d).start()
    for r in range(2):
        x_copy(1, r).start()
        own_copy(1, r).start()
    for d in NEAR:
        for r in range(2):
            gather_copy(1, r, 0, d).start()
    for load in loads:
        load.start()
    pairs = [(dx, d) for dx in range(2) for d in range(4) if dx or d]
    metadata(rt, gt, m1, m2)
    for r in range(2):
        mr[r, own[r], xh] = metas[r][xh, own[r]]
    for r in range(2):
        for dx, d in pairs:
            meta_copy(r, dx, d).start()

    def pass_on(a):
        for r in range(2):
            own_copy(a, r).wait()
            spot = ag.at[a, r, own[r], pl.ds((1 - xh) * 128, 128)]
            remote(spot, spot, xs.at[a, r], xr.at[a, r], partner).wait_recv()
            if a == 0:
                for d in NEAR:
                    gather_copy(a, r, 1, d).start()

    def cross_far(a):
        for r in range(2):
            for side in range(2):
                relay_wait(a, r, side)
            cross_copy(a, r, 2).start()

    relay(0)
    pass_on(0)
    cross_far(0)
    relay(1)
    for q in NEAR:
        for r in range(2):
            cross_copy(1, r, q).start()
    for r in range(2):
        for dx, d in pairs:
            meta_copy(r, dx, d).wait()

    def spread(a):
        def body(i, carry):
            q = turn(i)

            if a == 0:

                @pl.when(i == 1)
                def _():
                    for r in range(2):
                        for k in NEAR:
                            gather_wait(0, r, 1, k)

                @pl.when(i == 2)
                def _():
                    cross_far(1)

            for r in range(2):
                group = (own[r] + q) % 4

                if a == 0:

                    @pl.when(i == 3)
                    def _():
                        cross_wait(0, r, 2)

                else:

                    @pl.when(i > 0)
                    def _():
                        cross_wait(1, r, q)

                hit, share = selection(mr, r, group)
                hit = hit.astype(BF)
                for c in range(2):
                    part = pl.ds(c * (half // 2), half // 2)
                    rows = jnp.dot(hit, ag[a, r, group, :, part], preferred_element_type=F32)
                    if a == 1:
                        rows = rows * jnp.sum(share, axis=1, keepdims=True)
                    rows = rows.astype(BF)
                    for e in range(4):
                        sb[a, r, e, q, :, part] = rows[e * 80 : e * 80 + 80]
                for d in ORDER:
                    spread_copy(a, r, q, d).start()
                keep_copy(a, r, q).start()
            return carry

        lax.fori_loop(0, 4, body, 0)

    spread(0)
    pass_on(1)
    spread(1)
    results = (xo, yo)

    def landed(a, r, q):
        keep_copy(a, r, q).wait()
        for d in ORDER:
            spread_copy(a, r, q, d).wait()

    def leave(a, r):
        pltpu.make_async_copy(xb.at[a, r], results[a].at[r], os_.at[a, r]).start()

    for r in range(2):
        for q in range(4):
            landed(0, r, q)
        leave(0, r)
    for load in loads:
        load.wait()

    def stores(t):
        part = pl.ds(t * 320, 320)
        found = [
            pltpu.make_async_copy(acs.at[part], aco.at[part], fo.at[t, 0]),
        ]
        for r in range(2):
            found.append(pltpu.make_async_copy(prs.at[r, part], po.at[r, part], fo.at[t, 1 + r]))
        return found

    def forward(t, carry):
        part = pl.ds(t * 320, 320)
        both = jnp.dot(xb[0, 0, part], wgu[pl.ds(0, half)], preferred_element_type=F32)
        both = both + jnp.dot(xb[0, 1, part], wgu[pl.ds(half, half)], preferred_element_type=F32)
        both = both * scale_in
        gus[part] = both
        gate = both[:, :hidden]
        act = (gate * jax.nn.sigmoid(gate) * both[:, hidden:]).astype(BF)
        acs[part] = act
        for r in range(2):
            made = jnp.dot(act, wdn[:, pl.ds(r * half, half)], preferred_element_type=F32)
            prs[r, part] = (made * scale_hidden).astype(BF)
        for s in stores(t):
            s.start()
        return carry

    lax.fori_loop(0, 4, forward, 0)
    gas[...] = jnp.zeros_like(gas)
    inner = (((1,), (1,)), ((), ()))

    def leave_part(q, k):
        if k < 4:
            spot, r = pl.ds((k * 4 + (y + q) % 4) * 80, 80), 0
        else:
            spot, r = pl.ds(((z + q) % 4) * 320, 320), 1
        return pltpu.make_async_copy(xb.at[1, r, spot], yo.at[r, spot], lv.at[q, k])

    def grad_part(i, carry):
        q = turn(i)
        landed(1, 0, q)
        for k in range(4):
            leave_part(q, k).start()
        spots = [pl.ds((k * 4 + (y + q) % 4) * 80, 80) for k in range(4)]
        rows = jnp.concatenate([xb[1, 0, s] for s in spots], axis=0)
        more = lax.dot_general(rows, wdn[:, pl.ds(0, half)], inner, preferred_element_type=F32)
        for k, s in enumerate(spots):
            gas[s] += more[k * 80 : k * 80 + 80]
        landed(1, 1, q)
        leave_part(q, 4).start()
        part = pl.ds(((z + q) % 4) * 320, 320)
        gas[part] += lax.dot_general(
            xb[1, 1, part], wdn[:, pl.ds(half, half)], inner, preferred_element_type=F32
        )
        return carry

    lax.fori_loop(0, 4, grad_part, 0)
    mo[...] = mr[...]

    def grad_store(t):
        part = pl.ds(t * 160, 160)
        return pltpu.make_async_copy(grs.at[part], gro.at[part], go.at[t])

    def hidden_grads(t, carry):
        part = pl.ds(t * 160, 160)
        grad_act = gas[part] * scale_hidden
        gate = gus[part, pl.ds(0, hidden)]
        up = gus[part, pl.ds(hidden, hidden)]
        sig = jax.nn.sigmoid(gate)
        grs[part, pl.ds(0, hidden)] = (
            grad_act * up * sig * (1.0 + gate * (1.0 - sig))
        ).astype(BF)
        grs[part, pl.ds(hidden, hidden)] = (grad_act * gate * sig).astype(BF)
        grad_store(t).start()
        return carry

    lax.fori_loop(0, 8, hidden_grads, 0)
    for t in range(8):
        grad_store(t).wait()
    for r in range(2):
        cross_copy(0, r, 2).wait_send()
        for q in ORDER:
            cross_copy(1, r, q).wait_send()
    for t in range(4):
        for s in stores(t):
            s.wait()
    for a in range(2):
        for r in range(2):
            x_copy(a, r).wait_send()
            for h in range(2 - a):
                for d in NEAR:
                    gather_copy(a, r, h, d).wait_send()
            for side in range(2):
                relay_copy(a, r, side).wait_send()
            if a == 0:
                pltpu.make_async_copy(xb.at[a, r], results[a].at[r], os_.at[a, r]).wait()
    for q in range(4):
        for k in range(5):
            leave_part(q, k).wait()


def dispatch(tokens, cotangent, rt, gt, wg, wu, wd):
    rows, width = tokens.shape
    half = width // 2
    hidden = wd.shape[0]
    dma = pltpu.SemaphoreType.DMA
    anywhere = pl.BlockSpec(memory_space=pl.ANY)
    vmem = pl.BlockSpec(memory_space=pltpu.VMEM)
    slots = 32 * CAP
    halves = jax.ShapeDtypeStruct((2, slots, half), BF)
    return pl.pallas_call(
        dispatch_kernel,
        out_shape=(
            halves, halves, halves,
            jax.ShapeDtypeStruct((slots, hidden), BF),
            jax.ShapeDtypeStruct((slots, 2 * hidden), BF),
            jax.ShapeDtypeStruct((2, 4, 2, 8, 128), F32),
        ),
        in_specs=[anywhere, anywhere, vmem, vmem, anywhere, anywhere, anywhere],
        out_specs=(*[anywhere] * 5, vmem),
        scratch_shapes=[
            pltpu.VMEM((2, 2, 4, 256, half), BF),
            pltpu.VMEM((2, 2, 4, 4, 80, half), BF),
            pltpu.VMEM((2, 2, slots, half), BF),
            pltpu.VMEM((2, 4, 2, 8, 128), F32),
            pltpu.VMEM((2, 4, 8, 128), F32),
            pltpu.VMEM((2, 4, 8, 128), F32),
            pltpu.VMEM((width, 2 * hidden), BF),
            pltpu.VMEM((hidden, width), BF),
            pltpu.VMEM((slots, 2 * hidden), F32),
            pltpu.VMEM((slots, hidden), BF),
            pltpu.VMEM((2, slots, half), BF),
            pltpu.VMEM((slots, hidden), F32),
            pltpu.VMEM((slots, 2 * hidden), BF),
            dma((2, 2, 4)), dma((2, 2, 4)),
            dma((2, 2)), dma((2, 2)),
            dma((2, 2, 2, 4)), dma((2, 2, 2, 4)),
            dma((2, 2, 4, 4)), dma((2, 2, 4, 4)),
            dma((2, 2)), dma((2, 2, 4)), dma((2, 2)),
            dma((3,)), dma((4, 3)),
            dma((2, 2, 2)), dma((2, 2, 2)), dma((8,)),
            dma((2, 2, 4)), dma((2, 2, 4)), dma((4, 5)),
        ],
        compiler_params=pltpu.CompilerParams(
            collective_id=0, has_side_effects=True, vmem_limit_bytes=60 * 2**20
        ),
        name="dispatch",
    )(tokens, cotangent, rt, gt, wg, wu, wd)


def combine_kernel(
    bit, xi, yi, pr, aci, gri, mr, wg, wu, wd, mg, mu, md,
    out, tg, ngu_o, nd_o, mgu_o, md_o, bgu, bd,
    xv, yv, acv, grads, wgu, wdn, mgu, mdn, lgu, ldn, fgu, fdn,
    rb, qs, qr, xsend, xrecv, mine, kept,
    cs, cr, ls, ps, pt, xs, xr, ws, wr, wl, go, nl, av,
):
    xh, z, y = place()
    rep = lax.axis_index("replica")
    half = rb.shape[-1]
    hidden = wd.shape[0]
    scale_in = (2 * half) ** (-0.5)
    scale_hidden = hidden ** (-0.5)
    low, high = pl.ds(0, hidden), pl.ds(hidden, hidden)
    copies = [(gri, grads)]
    for k in range(2):
        rows = pl.ds(k * half, half)
        copies.append((xi.at[k], xv.at[k]))
        for src, dst, cols in ((mg, mgu, low), (mu, mgu, high), (wg, wgu, low), (wu, wgu, high)):
            copies.append((src.at[rows], dst.at[rows, cols]))
    copies += [(aci, acv), (yi, yv), (md, mdn), (wd, wdn)]
    loads = [pltpu.make_async_copy(s, d, wl.at[i]) for i, (s, d) in enumerate(copies)]
    for load in loads:
        load.start()
    own = (y, z)
    partner = {"expert": number(1 - xh, z, y)}
    core_mate = {"replica": rep + 1 - 2 * (rep % 2)}
    far_mate = {"replica": (rep + 2) % 4}
    others = [partner, core_mate, far_mate]
    for d in ORDER:
        others.append({"expert": number(xh, z, (y + d) % 4)})
        others.append({"expert": number(xh, (z + d) % 4, y)})
    greet(others)
    source = (pr, xv)
    results = (out, tg)

    def block(a, r, e, group):
        row = (e * 4 + group) if r == 0 else (group * 4 + e)
        return source[a].at[r, pl.ds(row * 80, 80)]

    def send_copy(a, r, q, d):
        group = (own[r] + q) % 4
        me = own[1 - r]
        return remote(
            block(a, r, (me + d) % 4, group), rb.at[a, r, group, me],
            cs.at[a, r, q, d], cr.at[a, r, q, d],
            {"expert": peer(r, 1, xh, z, y, d)},
        )

    def keep_copy(a, r, q):
        group = (own[r] + q) % 4
        me = own[1 - r]
        return pltpu.make_async_copy(block(a, r, me, group), rb.at[a, r, group, me], ls.at[a, r, q])

    def part_copy(a, r, q):
        return remote(
            qs.at[a, r, q - 1], qr.at[a, r, q - 1], ps.at[a, r, q], pt.at[a, r, q],
            {"expert": peer(r, 0, xh, z, y, q)},
        )

    def x_copy(a, r):
        return remote(xsend.at[a, r], xrecv.at[a, r], xs.at[a, r], xr.at[a, r], partner)

    def send_rows(a):
        for q in (1, 3, 2, 0):
            for r in range(2):
                keep_copy(a, r, q).start()
            for d in ORDER:
                for r in range(2):
                    send_copy(a, r, q, d).start()

    def in_tile(t):
        rows = pl.ds(t * 256, 256)
        src = lgu.at[rows]
        return [
            remote(src, fgu.at[rows], ws.at[1, t], wr.at[1, t], far_mate),
            remote(src, bgu.at[rows], ws.at[0, t], wr.at[0, t], core_mate),
        ]

    def down_tile(c):
        cols = pl.ds(c * 512, 512)
        src = ldn.at[:, cols]
        return [
            remote(src, fdn.at[:, cols], ws.at[1, 8 + c], wr.at[1, 8 + c], far_mate),
            remote(src, bd.at[:, cols], ws.at[0, 8 + c], wr.at[0, 8 + c], core_mate),
        ]

    send_rows(0)
    for load in loads[:6]:
        load.wait()
    outer = (((0,), (0,)), ((), ()))

    def in_grads(t, carry):
        @pl.when(t == 4)
        def _():
            for load in loads[6:11]:
                load.wait()

        rows = pl.ds(t * 256, 256)
        cols = pl.ds((t % 4) * 256, 256)
        grad = lax.dot_general(
            xv[t // 4, :, cols], grads[...], outer, preferred_element_type=F32
        ) * scale_in
        moment = momentum_beta * mgu[rows].astype(F32) + grad
        mgu[rows] = moment.astype(BF)
        lgu[rows] = (wgu[rows].astype(F32) - learn_rate * moment).astype(BF)
        for s in in_tile(t):
            s.start()
        return carry

    lax.fori_loop(0, 8, in_grads, 0)
    for load in loads[11:]:
        load.wait()

    def down_grads(c, carry):
        cols = pl.ds((c % 2) * 512, 512)
        where = pl.ds(c * 512, 512)
        grad = lax.dot_general(
            acv[...], yv[c // 2, :, cols], outer, preferred_element_type=F32
        ) * scale_hidden
        moment = momentum_beta * mdn[:, where].astype(F32) + grad
        mdn[:, where] = moment.astype(BF)
        ldn[:, where] = (wdn[:, where].astype(F32) - learn_rate * moment).astype(BF)
        for s in down_tile(c):
            s.start()
        return carry

    lax.fori_loop(0, 4, down_grads, 0)

    def back_rows(t, carry):
        part = pl.ds(t * 320, 320)
        inner = (((1,), (1,)), ((), ()))
        for r in range(2):
            back = lax.dot_general(
                grads[part], wgu[pl.ds(r * half, half)], inner, preferred_element_type=F32
            )
            xv[r, part] = (back * scale_in).astype(BF)
        return carry

    lax.fori_loop(0, 4, back_rows, 0)
    send_rows(1)
    moments = [
        pltpu.make_async_copy(s, d, go.at[i])
        for i, (s, d) in enumerate(((mgu, mgu_o), (mdn, md_o)))
    ]
    for m in moments:
        m.start()

    def reduce(a):
        def body(i, carry):
            q = turn((i + 1) % 4)
            for r in range(2):
                group = (own[r] + q) % 4
                keep_copy(a, r, q).wait()
                for d in ORDER:
                    send_copy(a, r, q, d).wait_recv()
                hit, share = selection(mr, r, group)
                pick = (share if a == 0 else hit).astype(BF)
                for c in range(2):
                    part = pl.ds(c * (half // 2), half // 2)
                    rows = jnp.concatenate([rb[a, r, group, e, :, part] for e in range(4)], axis=0)
                    total = lax.dot_general(pick, rows, outer, preferred_element_type=F32)

                    @pl.when(i < 3)
                    def _():
                        qs[a, r, (q + 3) % 4, :, part] = total.astype(BF)

                    @pl.when(i == 3)
                    def _():
                        mine[r, :, part] = total

                @pl.when(i < 3)
                def _():
                    part_copy(a, r, q).start()
            return carry

        lax.fori_loop(0, 4, body, 0)
        there = pl.ds((1 - xh) * 128, 128)
        here = pl.ds(xh * 128, 128)
        for r in range(2):
            for q in ORDER:
                part_copy(a, r, q).wait_recv()
            away = mine[r, there]
            stay = mine[r, here]
            for q in ORDER:
                away = away + qr[a, r, q - 1, there].astype(F32)
                stay = stay + qr[a, r, q - 1, here].astype(F32)
            xsend[a, r] = away.astype(BF)
            x_copy(a, r).start()
            kept[a, r] = stay

    reduce(0)
    for t in range(8):
        in_tile(t)[1].wait_recv()
    for c in range(4):
        down_tile(c)[1].wait_recv()
    near = [
        pltpu.make_async_copy(bgu, wgu, nl.at[0]),
        pltpu.make_async_copy(bd, wdn, nl.at[1]),
    ]
    for n in near:
        n.start()
    reduce(1)
    for n in near:
        n.wait()
    pick = bit[0] % 2 == 0

    def in_store(t):
        rows = pl.ds(t * 256, 256)
        return pltpu.make_async_copy(lgu.at[rows], ngu_o.at[rows], av.at[t])

    def down_store(c):
        cols = pl.ds(c * 512, 512)
        return pltpu.make_async_copy(ldn.at[:, cols], nd_o.at[:, cols], av.at[8 + c])

    def in_average(t, carry):
        far, close = in_tile(t)
        far.wait()
        close.wait_send()
        rows = pl.ds(t * 256, 256)
        other = jnp.where(pick, wgu[rows].astype(F32), fgu[rows].astype(F32))
        lgu[rows] = ((lgu[rows].astype(F32) + other) * 0.5).astype(BF)
        in_store(t).start()
        return carry

    def down_average(c, carry):
        far, close = down_tile(c)
        far.wait()
        close.wait_send()
        cols = pl.ds(c * 512, 512)
        other = jnp.where(pick, wdn[:, cols].astype(F32), fdn[:, cols].astype(F32))
        ldn[:, cols] = ((ldn[:, cols].astype(F32) + other) * 0.5).astype(BF)
        down_store(c).start()
        return carry

    lax.fori_loop(0, 8, in_average, 0)
    lax.fori_loop(0, 4, down_average, 0)
    for a in range(2):
        for r in range(2):
            x_copy(a, r).wait_recv()
            total = kept[a, r] + xrecv[a, r].astype(F32)
            results[a][:, pl.ds(r * half, half)] = total.astype(BF)
    for a in range(2):
        for r in range(2):
            x_copy(a, r).wait_send()
            for q in range(4):
                for d in ORDER:
                    send_copy(a, r, q, d).wait_send()
            for q in ORDER:
                part_copy(a, r, q).wait_send()
    for t in range(8):
        in_store(t).wait()
    for c in range(4):
        down_store(c).wait()
    for m in moments:
        m.wait()


def combine(bit, xi, yi, pr, aci, gri, mr, wg, wu, wd, mg, mu, md):
    half = xi.shape[2]
    width = 2 * half
    slots = xi.shape[1]
    hidden = wd.shape[0]
    dma = pltpu.SemaphoreType.DMA
    anywhere = pl.BlockSpec(memory_space=pl.ANY)
    vmem = pl.BlockSpec(memory_space=pltpu.VMEM)
    tokens = jax.ShapeDtypeStruct((128, width), BF)
    inward = jax.ShapeDtypeStruct((width, 2 * hidden), BF)
    down = jax.ShapeDtypeStruct((hidden, width), BF)
    return pl.pallas_call(
        combine_kernel,
        out_shape=(
            tokens, tokens, inward, down, inward, down, inward, down,
        ),
        in_specs=[pl.BlockSpec(memory_space=pltpu.SMEM), *[anywhere] * 5, vmem, *[anywhere] * 6],
        out_specs=(vmem, vmem, *[anywhere] * 6),
        scratch_shapes=[
            pltpu.VMEM((2, slots, half), BF),
            pltpu.VMEM((2, slots, half), BF),
            pltpu.VMEM((slots, hidden), BF),
            pltpu.VMEM((slots, 2 * hidden), BF),
            pltpu.VMEM((width, 2 * hidden), BF),
            pltpu.VMEM((hidden, width), BF),
            pltpu.VMEM((width, 2 * hidden), BF),
            pltpu.VMEM((hidden, width), BF),
            pltpu.VMEM((width, 2 * hidden), BF),
            pltpu.VMEM((hidden, width), BF),
            pltpu.VMEM((width, 2 * hidden), BF),
            pltpu.VMEM((hidden, width), BF),
            pltpu.VMEM((2, 2, 4, 4, 80, half), BF),
            pltpu.VMEM((2, 2, 3, 256, half), BF),
            pltpu.VMEM((2, 2, 3, 256, half), BF),
            pltpu.VMEM((2, 2, 128, half), BF),
            pltpu.VMEM((2, 2, 128, half), BF),
            pltpu.VMEM((2, 256, half), F32),
            pltpu.VMEM((2, 2, 128, half), F32),
            dma((2, 2, 4, 4)), dma((2, 2, 4, 4)),
            dma((2, 2, 4)),
            dma((2, 2, 4)), dma((2, 2, 4)),
            dma((2, 2)), dma((2, 2)),
            dma((2, 12)), dma((2, 12)),
            dma((15,)), dma((2,)), dma((2,)), dma((12,)),
        ],
        compiler_params=pltpu.CompilerParams(
            collective_id=1, has_side_effects=True, vmem_limit_bytes=63 * 2**20
        ),
        name="combine",
    )(bit, xi, yi, pr, aci, gri, mr, wg, wu, wd, mg, mu, md)


def finish_kernel(
    ngu, mgu, nd, md, out, tg, ngo, nuo, ndo, mgo, muo, mdo, oo, to,
    v0, v1, v2, v3, v4, v5, gets, puts,
):
    hidden = ngo.shape[1]
    whole = pl.ds(0, nd.shape[1])
    left, right = pl.ds(0, hidden), pl.ds(hidden, hidden)
    parts = 4
    pieces = []
    for k in range(parts):
        for src, buf, ends in (
            (ngu, v0, ((left, ngo), (right, nuo))), (mgu, v1, ((left, mgo), (right, muo))),
            (nd, v2, ((whole, ndo),)), (md, v3, ((whole, mdo),)),
            (out, v4, ((whole, oo),)), (tg, v5, ((whole, to),)),
        ):
            size = src.shape[0] // parts
            pieces.append((src, buf, pl.ds(k * size, size), ends))
    loads, stores = [], []
    for n, (src, buf, rows, ends) in enumerate(pieces):
        loads.append(pltpu.make_async_copy(src.at[rows], buf.at[rows], gets.at[n]))
        stores.append([
            pltpu.make_async_copy(buf.at[rows, cols], dst.at[rows], puts.at[n, i])
            for i, (cols, dst) in enumerate(ends)
        ])
    for load in loads:
        load.start()
    for load, ends in zip(loads, stores):
        load.wait()
        for store in ends:
            store.start()
    for ends in stores:
        for store in ends:
            store.wait()


def finish(ngu, mgu, nd, md, out, tg):
    width, both = ngu.shape
    hidden = both // 2
    shape = jax.ShapeDtypeStruct
    anywhere = pl.BlockSpec(memory_space=pl.ANY)
    inputs = (ngu, mgu, nd, md, out, tg)
    return pl.pallas_call(
        finish_kernel,
        out_shape=(
            shape((width, hidden), BF), shape((width, hidden), BF), shape((hidden, width), BF),
            shape((width, hidden), BF), shape((width, hidden), BF), shape((hidden, width), BF),
            shape((128, width), BF), shape((128, width), BF),
        ),
        in_specs=[anywhere] * 6,
        out_specs=(anywhere,) * 8,
        scratch_shapes=[
            *[pltpu.VMEM(v.shape, BF) for v in inputs],
            pltpu.SemaphoreType.DMA((24,)), pltpu.SemaphoreType.DMA((24, 2)),
        ],
        compiler_params=pltpu.CompilerParams(vmem_limit_bytes=62 * 2**20),
        name="finish",
    )(*inputs)


def per_device(
    tokens, routing, gate_scores, cotangent,
    w_gate, w_up, w_down, mom_gate, mom_up, mom_down, gossip_round,
):
    wg, wu, wd = w_gate[0, 0], w_up[0, 0], w_down[0, 0]
    xi, yi, pr, aci, gri, meta = dispatch(
        tokens, cotangent, routing.T, gate_scores.T, wg, wu, wd
    )
    out, tg, ngu, nd, mgu, md, _, _ = combine(
        gossip_round, xi, yi, pr, aci, gri, meta, wg, wu, wd,
        mom_gate[0, 0], mom_up[0, 0], mom_down[0, 0],
    )
    ng, nu, nd, mg, mu, mdn, layer_out, token_grad = finish(ngu, mgu, nd, md, out, tg)
    return (
        layer_out, token_grad, ng[None, None], nu[None, None], nd[None, None],
        mg[None, None], mu[None, None], mdn[None, None],
    )


def solution(mesh):
    flat = P(("replica", "expert"), None)
    stacked = P("replica", "expert", None, None)
    return jax.shard_map(
        per_device,
        mesh=mesh,
        in_specs=(flat,) * 4 + (stacked,) * 6 + (P("expert"),),
        out_specs=(flat,) * 2 + (stacked,) * 6,
        check_vma=False,
    )
```
